128 devices in a mesh: head: 2 (over y_hi), seq: 64 (over z, x, y_lo, core).
Axes of the slice: x: 4, y: 4 (y_hi: 2, y_lo: 2; y = y_hi * 2 + y_lo), z: 4, core: 2. Of those that a mesh axis runs over, the one named last changes fastest.
Arguments:
- queries: bfloat16 [65536, 2048], P('seq', 'head'), may hold values from -24 to 24
- key_rows: bfloat16 [65536, 2048], P('seq', 'head'), may hold values from -24 to 24
- value_rows: bfloat16 [65536, 2048], P('seq', 'head'), may hold values from -6 to 6
- token_rates: float32 [4, 65536], P('head', 'seq'), may hold values from 0.01 to 1
- gate_fast: float32 [4, 512, 512], P('head'), may hold values from -0.25 to 0.25
- lift_fast: float32 [4, 512, 512], P('head'), may hold values from -0.25 to 0.25
- down_fast: float32 [4, 512, 512], P('head'), may hold values from -0.25 to 0.25
- memory_gain: float32 [4, 512], P('head'), may hold values from 0.1 to 1
- out_weight: bfloat16 [2048, 2048], P('head'), may hold values from -0.125 to 0.125
Outputs:
- layer_out: bfloat16 [65536, 2048], P('seq', 'head')
The draws below stay inside these ranges and needn't reach their ends.
All inputs are finite; a program needn't handle non-finite values.
Results may differ from the reference program's by a relative error of at most 0.014.
Values may be sent and summed in bfloat16 or wider, within the bound.
No kernel may reach another device: no remote copies, remote signals or barrier semaphores. Data moves between devices by JAX's collectives and lax.ppermute only.
A program may use at most 128 MiB of HBM per device.

```python
import math
import jax
import jax.numpy as jnp
from jax import lax

HEADS = 4
HEAD = 512
FH = 512
D = 2048
WINDOW = 1024
NS_STEPS = 2
TOK_DEV = 1024
TOKENS = 65536


def shared_rows(key):
    base_key = jax.random.fold_in(key, 4099)
    split_keys = jax.random.split(base_key, 5)
    query_draw = jax.random.truncated_normal(split_keys[0], -4.0, 4.0, (TOKENS, HEADS, HEAD), jnp.float32)
    key_draw = jax.random.truncated_normal(split_keys[1], -4.0, 4.0, (TOKENS, HEADS, HEAD), jnp.float32)
    common_part = jax.random.uniform(split_keys[4], (1, HEADS, HEAD), jnp.float32, -0.8, 0.8)
    key_draw = key_draw + common_part
    return (query_draw.reshape(TOKENS, D), key_draw.reshape(TOKENS, D))


def draw_queries(key, part):
    return shared_rows(key)[0].astype(jnp.bfloat16)


def draw_key_rows(key, part):
    return shared_rows(key)[1].astype(jnp.bfloat16)


def block_scale(own_key, extent, shards, low, high):
    factor_of, own = 1.0, jax.random.fold_in(own_key, 6)
    for axis_at, blocks in shards:
        steps = jnp.exp(jax.random.uniform(jax.random.fold_in(own, axis_at), (blocks,), jnp.float32, low / len(shards), high / len(shards)))
        factor_of = factor_of * jnp.repeat(steps, extent[axis_at] // blocks).reshape([-1 if axis == axis_at else 1 for axis in range(len(extent))])
    return factor_of


def noise(rng, shape, spread, limit, pieces=(), held_as=jnp.bfloat16):
    values = jax.random.normal(rng, shape, jnp.float32) * spread
    if len(pieces) > 0:
        values = block_scale(rng, shape, pieces, -0.22, 0.18) * values
    return jnp.clip(values, min=-limit, max=limit).astype(held_as)


def setup_inputs(seed: int = 0) -> dict:
    key_list = jax.random.split(jax.random.key(seed), 10)
    return {
        "queries": draw_queries(jax.random.fold_in(key_list[9], 71), 0),
        "key_rows": draw_key_rows(jax.random.fold_in(key_list[9], 71), 0),
        "value_rows": noise(key_list[2], (TOKENS, D), 1.0, 6.0, ((0, 64), (1, 2))),
        "token_rates": jnp.clip(jnp.exp(math.log(1.0) - 4.6051702 * jax.random.uniform(key_list[3], (HEADS, TOKENS), jnp.float32) ** block_scale(key_list[3], (HEADS, TOKENS), ((0, 2), (1, 64)), -0.2, 0.2)), 0.01, 1.0),
        "gate_fast": noise(key_list[4], (HEADS, HEAD, FH), HEAD ** -0.5, 0.25, ((0, 2),), jnp.float32),
        "lift_fast": noise(key_list[5], (HEADS, HEAD, FH), HEAD ** -0.5, 0.25, ((0, 2),), jnp.float32),
        "down_fast": noise(key_list[6], (HEADS, FH, HEAD), FH ** -0.5, 0.25, ((0, 2),), jnp.float32),
        "memory_gain": jnp.clip(jnp.exp(math.log(1.0) - 2.3025851 * jax.random.uniform(key_list[7], (HEADS, HEAD), jnp.float32) ** block_scale(key_list[7], (HEADS, HEAD), ((0, 2),), -0.2, 0.2)), 0.1, 1.0),
        "out_weight": noise(key_list[8], (D, D), D ** -0.5, 0.125, ((0, 2),)),
    }


COEF_A = 3.4445
COEF_B = -4.775
COEF_C = 2.0315
EPSILON = 1e-06

def rounded(values_in):
    return lax.optimization_barrier(values_in.astype(jnp.bfloat16))

def window_attention(queries, key_rows, value_rows):
    total_rows = queries.shape[0]
    block_rows = min(512, TOK_DEV)
    span_rows = block_rows + WINDOW
    padding = jnp.zeros((WINDOW, D), jnp.bfloat16)
    all_keys = jnp.concatenate([padding, key_rows], axis=0)
    all_values = jnp.concatenate([padding, value_rows], axis=0)
    score_scale = HEAD ** (-0.5)
    query_index = jnp.arange(block_rows, dtype=jnp.int32)[:, None]
    key_index = jnp.arange(span_rows, dtype=jnp.int32)[None, :]

    def one_block(start):
        query_block = lax.dynamic_slice_in_dim(queries, start, block_rows, 0).reshape(block_rows, HEADS, HEAD).astype(jnp.float32)
        key_block = lax.dynamic_slice_in_dim(all_keys, start, span_rows, 0).reshape(span_rows, HEADS, HEAD).astype(jnp.float32)
        value_block = lax.dynamic_slice_in_dim(all_values, start, span_rows, 0).reshape(span_rows, HEADS, HEAD).astype(jnp.float32)
        scores = jnp.einsum('qhd,khd->hqk', query_block, key_block) * score_scale
        allowed = (key_index > query_index) & (key_index <= query_index + WINDOW) & (start + key_index - WINDOW >= 0)
        scores = jnp.where(allowed[None, :, :], scores, -jnp.inf)
        largest = lax.optimization_barrier(jnp.max(scores, axis=2, keepdims=True))
        exponent = jnp.exp(scores - largest)
        probability = rounded(exponent / lax.optimization_barrier(jnp.sum(exponent, axis=2, keepdims=True))).astype(jnp.float32)
        attended = jnp.einsum('hqk,khd->qhd', probability, value_block)
        return attended.reshape(block_rows, D)
    starts = jnp.arange(total_rows // block_rows, dtype=jnp.int32) * block_rows
    return lax.map(one_block, starts).reshape(total_rows, D)

def orthogonal(gradient):
    column_gram = jnp.dot(gradient.T, gradient, precision=lax.Precision.HIGHEST)
    trace_sum = jnp.trace(column_gram) + EPSILON
    iterate = (gradient / jnp.sqrt(trace_sum)).astype(jnp.bfloat16)
    column_gram = column_gram / trace_sum
    identity = jnp.eye(column_gram.shape[0], dtype=jnp.float32)
    for sweep_index in range(NS_STEPS):
        gram_half = column_gram.astype(jnp.bfloat16)
        square = jnp.dot(gram_half, gram_half, preferred_element_type=jnp.float32)
        polynomial = (COEF_A * identity + COEF_B * column_gram + COEF_C * square).astype(jnp.bfloat16)
        iterate = jnp.dot(iterate, polynomial, preferred_element_type=jnp.float32).astype(jnp.bfloat16)
        if sweep_index + 1 < NS_STEPS:
            column_gram = jnp.dot(iterate.T, iterate, preferred_element_type=jnp.float32)
    return iterate

def renew(old_weight, update):
    change = old_weight - update.astype(jnp.float32)
    old_square = lax.optimization_barrier(jnp.sum(old_weight * old_weight, axis=0, keepdims=True))
    new_square = lax.optimization_barrier(jnp.sum(change * change, axis=0, keepdims=True))
    return (change * jnp.sqrt(old_square / (new_square + EPSILON))).astype(jnp.bfloat16)

def head_memory(key_head, value_head, query_head, rate_head, gate_fast, lift_fast, down_fast, memory_gain):
    gate_pre = jnp.dot(key_head, rounded(gate_fast), preferred_element_type=jnp.float32)
    lift_pre = jnp.dot(key_head, rounded(lift_fast), preferred_element_type=jnp.float32)
    sigmoid_gate = jax.nn.sigmoid(gate_pre)
    activated = gate_pre * sigmoid_gate
    hidden = (activated * lift_pre).astype(jnp.bfloat16)
    target = (-rate_head[:, None] * value_head.astype(jnp.float32)).astype(jnp.bfloat16)
    grad_down = jnp.dot(hidden.T, target, preferred_element_type=jnp.float32)
    back_hidden = jnp.dot(target, rounded(down_fast).T, preferred_element_type=jnp.float32)
    back_gate = (back_hidden * lift_pre * sigmoid_gate * (1.0 + gate_pre * (1.0 - sigmoid_gate))).astype(jnp.bfloat16)
    back_lift = (back_hidden * activated).astype(jnp.bfloat16)
    grad_gate = jnp.dot(key_head.T, back_gate, preferred_element_type=jnp.float32)
    grad_lift = jnp.dot(key_head.T, back_lift, preferred_element_type=jnp.float32)
    gate_new = renew(gate_fast, orthogonal(grad_gate))
    lift_new = renew(lift_fast, orthogonal(grad_lift))
    down_new = renew(down_fast, orthogonal(grad_down))
    gate_apply = jnp.dot(query_head, gate_new, preferred_element_type=jnp.float32)
    lift_apply = jnp.dot(query_head, lift_new, preferred_element_type=jnp.float32)
    hidden_apply = (jax.nn.silu(gate_apply) * lift_apply).astype(jnp.bfloat16)
    memory_out = jnp.dot(hidden_apply, down_new, preferred_element_type=jnp.float32)
    mean_square = lax.optimization_barrier(jnp.mean(memory_out * memory_out, axis=1, keepdims=True))
    return memory_out * lax.rsqrt(mean_square + EPSILON) * memory_gain[None, :]

def reference(queries, key_rows, value_rows, token_rates, gate_fast, lift_fast, down_fast, memory_gain, out_weight):
    attended = window_attention(queries, key_rows, value_rows)
    query_heads = queries.reshape(TOKENS, HEADS, HEAD).transpose(1, 0, 2)
    key_heads = key_rows.reshape(TOKENS, HEADS, HEAD).transpose(1, 0, 2)
    value_heads = value_rows.reshape(TOKENS, HEADS, HEAD).transpose(1, 0, 2)

    def one_head(items):
        return head_memory(items[0], items[1], items[2], items[3], items[4], items[5], items[6], items[7])
    memory = lax.map(one_head, (key_heads, value_heads, query_heads, token_rates, gate_fast, lift_fast, down_fast, memory_gain))
    memory_flat = memory.transpose(1, 0, 2).reshape(TOKENS, D)
    combined = (attended + memory_flat).astype(jnp.bfloat16)
    return jnp.dot(combined, out_weight, preferred_element_type=jnp.float32).astype(jnp.bfloat16)
```

```python
import jax
import jax.numpy as jnp
from jax import lax
from jax.experimental import pallas as pl
from jax.experimental.pallas import tpu as pltpu
from jax.sharding import PartitionSpec as P

HEAD = 512
WINDOW = 1024
NS_STEPS = 2
COEF_A = 3.4445
COEF_B = -4.775
COEF_C = 2.0315
EPSILON = 1e-06

CHUNK = 256
BF = jnp.bfloat16
F32 = jnp.float32
MIB = 1 << 20

PLANE = 4
PLANES = 16

ROW_BY_ROW = (((1,), (1,)), ((), ()))
COL_BY_COL = (((0,), (0,)), ((), ()))


def dot(a, b):
    return jnp.dot(a, b, preferred_element_type=F32)


def dot_on(a, b, dims):
    return lax.dot_general(a, b, dims, preferred_element_type=F32)


def any_spec():
    return pl.BlockSpec(memory_space=pl.ANY)


def sigmoid(x):
    return 1.0 / (1.0 + jnp.exp(-x))


def grads_body(where, k_ref, v_ref, rate_ref, gate_ref, lift_ref, down_ref, out_ref, acc, w16):
    step = pl.program_id(0)

    @pl.when(step == 0)
    def _():
        w16[0] = gate_ref[0].astype(BF)
        w16[1] = lift_ref[0].astype(BF)
        w16[2] = down_ref[0].astype(BF)
        acc[...] = jnp.zeros_like(acc)

    keys = k_ref[...]
    rates = jnp.where(where[0] == 0, rate_ref[0:1, :], rate_ref[1:2, :])
    rate_col = jnp.broadcast_to(rates, (128, rates.shape[1])).T[:, :1]
    target = (-rate_col * v_ref[...].astype(F32)).astype(BF)
    gate_pre = dot(keys, w16[0])
    lift_pre = dot(keys, w16[1])
    back_hidden = dot_on(target, w16[2], ROW_BY_ROW)
    sig = sigmoid(gate_pre)
    activated = gate_pre * sig
    hidden = (activated * lift_pre).astype(BF)
    back_gate = (back_hidden * lift_pre * sig * (1.0 + gate_pre * (1.0 - sig))).astype(BF)
    back_lift = (back_hidden * activated).astype(BF)
    acc[0] += dot_on(keys, back_gate, COL_BY_COL)
    acc[1] += dot_on(keys, back_lift, COL_BY_COL)
    acc[2] += dot_on(hidden, target, COL_BY_COL)

    @pl.when(step == pl.num_programs(0) - 1)
    def _():
        for i in range(3):
            out_ref[i * HEAD : (i + 1) * HEAD, :] = acc[i].astype(out_ref.dtype)


def head_grads(which, keys, values, rates, gate, lift, down, dtype):
    tokens = keys.shape[0]
    rows = 256
    weight = pl.BlockSpec((1, HEAD, HEAD), lambda i, w: (w[0], 0, 0))
    token = pl.BlockSpec((rows, HEAD), lambda i, w: (i, w[0]))
    return pl.pallas_call(
        grads_body,
        out_shape=jax.ShapeDtypeStruct((3 * HEAD, HEAD), dtype),
        grid_spec=pltpu.PrefetchScalarGridSpec(
            num_scalar_prefetch=1,
            grid=(tokens // rows,),
            in_specs=[
                token,
                token,
                pl.BlockSpec((2, rows), lambda i, w: (0, i)),
                weight,
                weight,
                weight,
            ],
            out_specs=pl.BlockSpec((3 * HEAD, HEAD), lambda i, w: (0, 0)),
            scratch_shapes=[pltpu.VMEM((3, HEAD, HEAD), F32), pltpu.VMEM((3, HEAD, HEAD), BF)],
        ),
        compiler_params=pltpu.CompilerParams(
            dimension_semantics=("arbitrary",), vmem_limit_bytes=32 * MIB
        ),
        name="head_grads",
    )(which, keys, values, rates, gate, lift, down)


def renew_body(where, g_ref, gate_ref, lift_ref, down_ref, out_ref):
    eye = (
        lax.broadcasted_iota(jnp.int32, (HEAD, HEAD), 0)
        == lax.broadcasted_iota(jnp.int32, (HEAD, HEAD), 1)
    ).astype(F32)
    olds = (gate_ref, lift_ref, down_ref)
    iterates, grams = [], []
    for i in range(3):
        g = g_ref[i * HEAD : (i + 1) * HEAD, :]
        wide = g.astype(F32)
        gram = dot_on(g, g, COL_BY_COL)
        squares = jnp.sum(wide * wide, axis=0, keepdims=True)
        inverse = lax.rsqrt(jnp.sum(squares, axis=1, keepdims=True) + EPSILON)
        iterates.append((wide * inverse).astype(BF))
        grams.append(gram * (inverse * inverse))
    for sweep in range(NS_STEPS):
        polys = []
        for i in range(3):
            half = grams[i].astype(BF)
            square = dot(half, half)
            polys.append((COEF_A * eye + COEF_B * grams[i] + COEF_C * square).astype(BF))
        for i in range(3):
            iterates[i] = dot(iterates[i], polys[i]).astype(BF)
        if sweep + 1 < NS_STEPS:
            for i in range(3):
                grams[i] = dot_on(iterates[i], iterates[i], COL_BY_COL)
    for i in range(3):
        old = olds[i][0]
        change = old - iterates[i].astype(F32)
        old_square = jnp.sum(old * old, axis=0, keepdims=True)
        new_square = jnp.sum(change * change, axis=0, keepdims=True)
        out_ref[i * HEAD : (i + 1) * HEAD, :] = (
            change * jnp.sqrt(old_square / (new_square + EPSILON))
        ).astype(BF)


def renewed_weights(which, grads, gate, lift, down):
    weight = pl.BlockSpec((1, HEAD, HEAD), lambda i, w: (w[0], 0, 0))
    whole = pl.BlockSpec((3 * HEAD, HEAD), lambda i, w: (0, 0))
    return pl.pallas_call(
        renew_body,
        out_shape=jax.ShapeDtypeStruct((3 * HEAD, HEAD), BF),
        grid_spec=pltpu.PrefetchScalarGridSpec(
            num_scalar_prefetch=1,
            grid=(1,),
            in_specs=[whole, weight, weight, weight],
            out_specs=whole,
        ),
        compiler_params=pltpu.CompilerParams(vmem_limit_bytes=48 * MIB),
        name="renewed_weights",
    )(which, grads, gate, lift, down)


def attention_chunk(at, has_edge, queries, keys, values, edge_keys, edge_values, after):
    blocks = WINDOW // CHUNK
    total = blocks + 1
    from_edge = blocks - at
    scale = HEAD ** (-0.5)

    def body(flag, q_ref, *refs):
        k_refs, v_refs, out_ref = refs[:total], refs[total : 2 * total], refs[-1]
        q = q_ref[...]
        row = lax.broadcasted_iota(jnp.int32, (CHUNK, CHUNK), 0)
        col = lax.broadcasted_iota(jnp.int32, (CHUNK, CHUNK), 1)
        scores = [dot_on(q, k_refs[j][...], ROW_BY_ROW) for j in range(total)]
        scores[0] = jnp.where(col > row, scores[0], -jnp.inf)
        scores[-1] = jnp.where(col <= row, scores[-1], -jnp.inf)
        edge_on = flag[0] > 0

        def rowmax(parts):
            best = parts[0]
            for part in parts[1:]:
                best = jnp.maximum(best, part)
            return jnp.max(best, axis=1, keepdims=True)

        own_max = rowmax(scores[from_edge:])
        both_max = jnp.maximum(own_max, rowmax(scores[:from_edge]))
        largest = jnp.where(edge_on, both_max, own_max)
        edge_largest = jnp.where(edge_on, both_max, jnp.inf)
        weights = [
            jnp.exp((scores[j] - (edge_largest if j < from_edge else largest)) * scale)
            for j in range(total)
        ]
        together = weights[0]
        for part in weights[1:]:
            together = together + part
        summed = jnp.sum(together, axis=1, keepdims=True)
        mixed = dot(weights[0].astype(BF), v_refs[0][...])
        for j in range(1, total):
            mixed = mixed + dot(weights[j].astype(BF), v_refs[j][...])
        out_ref[...] = mixed / summed

    def spec(row):
        return pl.BlockSpec((CHUNK, HEAD), lambda h, flag: (row, h))

    rows = [spec(at + j) for j in range(from_edge)] + [spec(j) for j in range(at + 1)]
    key_args = [edge_keys] * from_edge + [keys] * (at + 1)
    value_args = [edge_values] * from_edge + [values] * (at + 1)
    width = queries.shape[1]
    return pl.pallas_call(
        body,
        out_shape=jax.ShapeDtypeStruct((CHUNK, width), F32),
        grid_spec=pltpu.PrefetchScalarGridSpec(
            num_scalar_prefetch=1,
            grid=(width // HEAD,),
            in_specs=[spec(at)] + rows + rows + [any_spec()] * len(after),
            out_specs=pl.BlockSpec((CHUNK, HEAD), lambda h, flag: (0, h)),
        ),
        compiler_params=pltpu.CompilerParams(vmem_limit_bytes=32 * MIB),
        name=f"attention_{at}",
    )(has_edge, queries, *key_args, *value_args, *after)


def tail_body(where, q0, q1, a0, a1, w0, w1, gain, s0, s1, o0, o1, send_ref, own_ref):
    combined = []
    for q_ref, a_ref, w_ref, head in ((q0, a0, w0, where[0]), (q1, a1, w1, 1 - where[0])):
        q = q_ref[...]
        gate = dot(q, w_ref[0:HEAD, :])
        lift = dot(q, w_ref[HEAD : 2 * HEAD, :])
        hidden = (gate * sigmoid(gate) * lift).astype(BF)
        out = dot(hidden, w_ref[2 * HEAD :, :])
        mean_square = jnp.mean(out * out, axis=1, keepdims=True)
        scale = jnp.where(head == 0, gain[0:1, :], gain[1:2, :])
        combined.append((a_ref[...] + out * lax.rsqrt(mean_square + EPSILON) * scale).astype(BF))
    send_ref[...] = (dot(combined[0], s0[...]) + dot(combined[1], s1[...])).astype(BF)
    own_ref[...] = dot(combined[0], o0[...]) + dot(combined[1], o1[...])


def tail_chunk(at, where, queries, attended, mine, theirs, gain, out_weight):
    width = queries.shape[1]
    columns = out_weight.shape[1] // 2
    whole = pl.BlockSpec((3 * HEAD, HEAD), lambda i, w: (0, 0))

    def token(row, mirror):
        return pl.BlockSpec((CHUNK, HEAD), lambda i, w: (row, 1 - w[0] if mirror else w[0]))

    def out_rows(mirror, send):
        return pl.BlockSpec(
            (HEAD, columns),
            lambda i, w: (1 - w[0] if mirror else w[0], 1 - w[1] if send else w[1]),
        )

    block = pl.BlockSpec((CHUNK, columns), lambda i, w: (0, 0))
    return pl.pallas_call(
        tail_body,
        out_shape=(
            jax.ShapeDtypeStruct((CHUNK, columns), BF),
            jax.ShapeDtypeStruct((CHUNK, columns), F32),
        ),
        grid_spec=pltpu.PrefetchScalarGridSpec(
            num_scalar_prefetch=1,
            grid=(1,),
            in_specs=[
                token(at, False),
                token(at, True),
                token(0, False),
                token(0, True),
                whole,
                whole,
                pl.BlockSpec((2, HEAD), lambda i, w: (0, 0)),
                out_rows(False, True),
                out_rows(True, True),
                out_rows(False, False),
                out_rows(True, False),
            ],
            out_specs=[block, block],
        ),
        compiler_params=pltpu.CompilerParams(vmem_limit_bytes=40 * MIB),
        name=f"tail_{at}",
    )(
        where,
        queries,
        queries,
        attended,
        attended,
        mine,
        theirs,
        gain,
        out_weight,
        out_weight,
        out_weight,
        out_weight,
    )


def finish_chunk(at, chunks, own, arrived, before):
    columns = own.shape[1]

    def body(own_ref, arrived_ref, *refs):
        refs[-1][...] = (own_ref[...] + arrived_ref[...].astype(F32)).astype(BF)

    block = pl.BlockSpec((CHUNK, columns), lambda i: (0, 0))
    held = () if before is None else (before,)
    return pl.pallas_call(
        body,
        out_shape=jax.ShapeDtypeStruct((chunks * CHUNK, columns), BF),
        grid=(1,),
        in_specs=[block, block] + [any_spec()] * len(held),
        out_specs=pl.BlockSpec((CHUNK, columns), lambda i: (at, 0)),
        input_output_aliases={2: 0} if held else {},
        name=f"finish_{at}",
    )(own, arrived, *held)


def partner(value, flip):
    count = lax.axis_size("seq")
    return lax.ppermute(value, "seq", [(i, i ^ flip) for i in range(count)])


def over_planes(value):
    groups = [[p * PLANE + r for p in range(PLANES)] for r in range(PLANE)]
    return lax.all_to_all(value, "seq", 0, 0, tiled=True, axis_index_groups=groups)


def shards(
    queries,
    key_rows,
    value_rows,
    token_rates,
    gate_fast,
    lift_fast,
    down_fast,
    memory_gain,
    out_weight,
):
    tokens_here = queries.shape[0]
    chunks = tokens_here // CHUNK
    seq = lax.axis_index("seq")
    core = (seq % 2).astype(jnp.int32)
    head = lax.axis_index("head").astype(jnp.int32)
    where = jnp.stack([core, head])
    mirrored = jnp.stack([1 - core, head])
    has_edge = jnp.where(seq > 0, 1, 0).astype(jnp.int32).reshape(1)

    fast = (gate_fast, lift_fast, down_fast)
    tokens = (key_rows, value_rows, token_rates)
    grads_send = head_grads(mirrored, *tokens, *fast, BF)
    grads_got = partner(grads_send, 1)
    grads_mine = head_grads(where, *tokens, *fast, F32)

    count = lax.axis_size("seq")
    along = [(i, i + 1) for i in range(count - 1)]
    edge_keys, edge_values = lax.ppermute((key_rows, value_rows), "seq", along)

    chip_sum = (grads_mine + grads_got.astype(F32)).astype(BF)
    slices = over_planes(chip_sum.reshape(PLANES, -1, HEAD))
    part = slices.astype(F32).sum(axis=0).astype(BF)
    other = partner(part, 2)
    part = (part.astype(F32) + other.astype(F32)).astype(BF)
    spread = jnp.broadcast_to(part[None], (PLANES, *part.shape))
    grads = over_planes(spread).reshape(3 * HEAD, HEAD)

    weights_mine = renewed_weights(where, grads, *fast)
    weights_theirs = partner(weights_mine, 1)

    head_pair = [(0, 1), (1, 0)]
    owns, arrivals = [], []
    after = ()
    for at in range(chunks):
        if at == 1:
            after = (weights_mine,)
        attended = attention_chunk(
            at, has_edge, queries, key_rows, value_rows, edge_keys, edge_values, after
        )
        send, own = tail_chunk(
            at, where, queries, attended, weights_mine, weights_theirs, memory_gain, out_weight
        )
        owns.append(own)
        arrivals.append(lax.ppermute(send, "head", head_pair))
        after = (send,)
    out = None
    for at in range(chunks):
        out = finish_chunk(at, chunks, owns[at], arrivals[at], out)
    return out


def solution(mesh):
    return jax.shard_map(
        shards,
        mesh=mesh,
        in_specs=(
            P("seq", "head"),
            P("seq", "head"),
            P("seq", "head"),
            P("head", "seq"),
            P("head", None, None),
            P("head", None, None),
            P("head", None, None),
            P("head", None),
            P("head", None),
        ),
        out_specs=P("seq", "head"),
        check_vma=False,
    )
```

```python
import jax
import jax.numpy as jnp
from jax import lax
from jax.experimental import pallas as pl
from jax.experimental.pallas import tpu as pltpu
from jax.sharding import PartitionSpec as P


HEAD = 512
WINDOW = 1024
NS_STEPS = 2
COEF_A = 3.4445
COEF_B = -4.775
COEF_C = 2.0315
EPSILON = 1e-06

CHUNK = 256
BF = jnp.bfloat16
F32 = jnp.float32
MIB = 1 << 20

PLANE = 4
PLANES = 16

ROW_BY_ROW = (((1,), (1,)), ((), ()))
COL_BY_COL = (((0,), (0,)), ((), ()))


def dot(a, b):
    return jnp.dot(a, b, preferred_element_type=F32)


def dot_on(a, b, dims):
    return lax.dot_general(a, b, dims, preferred_element_type=F32)


def any_spec():
    return pl.BlockSpec(memory_space=pl.ANY)


def sigmoid(x):
    return 1.0 / (1.0 + jnp.exp(-x))


def grads_body(where, k_ref, v_ref, rate_ref, gate_ref, lift_ref, down_ref, out_ref, acc, w16):
    step = pl.program_id(0)

    @pl.when(step == 0)
    def _():
        w16[0] = gate_ref[0].astype(BF)
        w16[1] = lift_ref[0].astype(BF)
        w16[2] = down_ref[0].astype(BF)
        acc[...] = jnp.zeros_like(acc)

    keys = k_ref[...]
    rates = jnp.where(where[0] == 0, rate_ref[0:1, :], rate_ref[1:2, :])
    rate_col = jnp.broadcast_to(rates, (128, rates.shape[1])).T[:, :1]
    target = (-rate_col * v_ref[...].astype(F32)).astype(BF)
    gate_pre = dot(keys, w16[0])
    lift_pre = dot(keys, w16[1])
    back_hidden = dot_on(target, w16[2], ROW_BY_ROW)
    sig = sigmoid(gate_pre)
    activated = gate_pre * sig
    hidden = (activated * lift_pre).astype(BF)
    back_gate = (back_hidden * lift_pre * sig * (1.0 + gate_pre * (1.0 - sig))).astype(BF)
    back_lift = (back_hidden * activated).astype(BF)
    acc[0] += dot_on(keys, back_gate, COL_BY_COL)
    acc[1] += dot_on(keys, back_lift, COL_BY_COL)
    acc[2] += dot_on(hidden, target, COL_BY_COL)

    @pl.when(step == pl.num_programs(0) - 1)
    def _():
        for i in range(3):
            out_ref[i * HEAD : (i + 1) * HEAD, :] = acc[i].astype(out_ref.dtype)


def head_grads(which, keys, values, rates, gate, lift, down, dtype):
    tokens = keys.shape[0]
    rows = 256
    weight = pl.BlockSpec((1, HEAD, HEAD), lambda i, w: (w[0], 0, 0))
    token = pl.BlockSpec((rows, HEAD), lambda i, w: (i, w[0]))
    return pl.pallas_call(
        grads_body,
        out_shape=jax.ShapeDtypeStruct((3 * HEAD, HEAD), dtype),
        grid_spec=pltpu.PrefetchScalarGridSpec(
            num_scalar_prefetch=1,
            grid=(tokens // rows,),
            in_specs=[
                token,
                token,
                pl.BlockSpec((2, rows), lambda i, w: (0, i)),
                weight,
                weight,
                weight,
            ],
            out_specs=pl.BlockSpec((3 * HEAD, HEAD), lambda i, w: (0, 0)),
            scratch_shapes=[pltpu.VMEM((3, HEAD, HEAD), F32), pltpu.VMEM((3, HEAD, HEAD), BF)],
        ),
        compiler_params=pltpu.CompilerParams(
            dimension_semantics=("arbitrary",), vmem_limit_bytes=32 * MIB
        ),
        name="head_grads",
    )(which, keys, values, rates, gate, lift, down)


def renew_body(where, g_ref, gate_ref, lift_ref, down_ref, out_ref, olds, sems):
    copies = [
        pltpu.make_async_copy(ref.at[where[0]], olds.at[i], sems.at[i])
        for i, ref in enumerate((gate_ref, lift_ref, down_ref))
    ]
    for copy in copies:
        copy.start()
    eye = (
        lax.broadcasted_iota(jnp.int32, (HEAD, HEAD), 0)
        == lax.broadcasted_iota(jnp.int32, (HEAD, HEAD), 1)
    ).astype(F32)
    iterates, grams = [], []
    for i in range(3):
        g = g_ref[i * HEAD : (i + 1) * HEAD, :]
        wide = g.astype(F32)
        gram = dot_on(g, g, COL_BY_COL)
        squares = jnp.sum(wide * wide, axis=0, keepdims=True)
        inverse = lax.rsqrt(jnp.sum(squares, axis=1, keepdims=True) + EPSILON)
        iterates.append((wide * inverse).astype(BF))
        grams.append(gram * (inverse * inverse))
    for sweep in range(NS_STEPS):
        polys = []
        for i in range(3):
            half = grams[i].astype(BF)
            square = dot(half, half)
            polys.append((COEF_A * eye + COEF_B * grams[i] + COEF_C * square).astype(BF))
        for i in range(3):
            iterates[i] = dot(iterates[i], polys[i]).astype(BF)
        if sweep + 1 < NS_STEPS:
            for i in range(3):
                grams[i] = dot_on(iterates[i], iterates[i], COL_BY_COL)
    for i in range(3):
        copies[i].wait()
        old = olds[i]
        change = old - iterates[i].astype(F32)
        old_square = jnp.sum(old * old, axis=0, keepdims=True)
        new_square = jnp.sum(change * change, axis=0, keepdims=True)
        out_ref[i * HEAD : (i + 1) * HEAD, :] = (
            change * jnp.sqrt(old_square / (new_square + EPSILON))
        ).astype(BF)


def renewed_weights(which, grads, gate, lift, down):
    whole = pl.BlockSpec((3 * HEAD, HEAD), lambda i, w: (0, 0))
    return pl.pallas_call(
        renew_body,
        out_shape=jax.ShapeDtypeStruct((3 * HEAD, HEAD), BF),
        grid_spec=pltpu.PrefetchScalarGridSpec(
            num_scalar_prefetch=1,
            grid=(1,),
            in_specs=[whole, any_spec(), any_spec(), any_spec()],
            out_specs=whole,
            scratch_shapes=[pltpu.VMEM((3, HEAD, HEAD), F32), pltpu.SemaphoreType.DMA((3,))],
        ),
        compiler_params=pltpu.CompilerParams(vmem_limit_bytes=48 * MIB),
        name="renewed_weights",
    )(which, grads, gate, lift, down)


def attention_chunk(at, has_edge, queries, keys, values, edge_keys, edge_values, after):
    blocks = WINDOW // CHUNK
    total = blocks + 1
    from_edge = blocks - at
    scale = HEAD ** (-0.5)

    def body(flag, q_ref, *refs):
        k_refs, v_refs, out_ref = refs[:total], refs[total : 2 * total], refs[-1]
        q = q_ref[...]
        row = lax.broadcasted_iota(jnp.int32, (CHUNK, CHUNK), 0)
        col = lax.broadcasted_iota(jnp.int32, (CHUNK, CHUNK), 1)
        scores = [dot_on(q, k_refs[j][...], ROW_BY_ROW) for j in range(total)]
        scores[0] = jnp.where(col > row, scores[0], -jnp.inf)
        scores[-1] = jnp.where(col <= row, scores[-1], -jnp.inf)
        edge_on = flag[0] > 0

        def rowmax(parts):
            best = parts[0]
            for part in parts[1:]:
                best = jnp.maximum(best, part)
            return jnp.max(best, axis=1, keepdims=True)

        own_max = rowmax(scores[from_edge:])
        both_max = jnp.maximum(own_max, rowmax(scores[:from_edge]))
        largest = jnp.where(edge_on, both_max, own_max)
        edge_largest = jnp.where(edge_on, both_max, jnp.inf)
        weights = [
            jnp.exp((scores[j] - (edge_largest if j < from_edge else largest)) * scale)
            for j in range(total)
        ]
        together = weights[0]
        for part in weights[1:]:
            together = together + part
        summed = jnp.sum(together, axis=1, keepdims=True)
        mixed = dot(weights[0].astype(BF), v_refs[0][...])
        for j in range(1, total):
            mixed = mixed + dot(weights[j].astype(BF), v_refs[j][...])
        out_ref[...] = mixed / summed

    def spec(row):
        return pl.BlockSpec((CHUNK, HEAD), lambda h, flag: (row, h))

    rows = [spec(at + j) for j in range(from_edge)] + [spec(j) for j in range(at + 1)]
    key_args = [edge_keys] * from_edge + [keys] * (at + 1)
    value_args = [edge_values] * from_edge + [values] * (at + 1)
    width = queries.shape[1]
    return pl.pallas_call(
        body,
        out_shape=jax.ShapeDtypeStruct((CHUNK, width), F32),
        grid_spec=pltpu.PrefetchScalarGridSpec(
            num_scalar_prefetch=1,
            grid=(width // HEAD,),
            in_specs=[spec(at)] + rows + rows + [any_spec()] * len(after),
            out_specs=pl.BlockSpec((CHUNK, HEAD), lambda h, flag: (0, h)),
        ),
        compiler_params=pltpu.CompilerParams(vmem_limit_bytes=32 * MIB),
    )(has_edge, queries, *key_args, *value_args, *after)


def tail_body(where, q0, q1, a0, a1, w0, w1, gain, s0, s1, o0, o1, send_ref, own_ref):
    combined = []
    for q_ref, a_ref, w_ref, head in ((q0, a0, w0, where[0]), (q1, a1, w1, 1 - where[0])):
        q = q_ref[...]
        gate = dot(q, w_ref[0:HEAD, :])
        lift = dot(q, w_ref[HEAD : 2 * HEAD, :])
        hidden = (gate * sigmoid(gate) * lift).astype(BF)
        out = dot(hidden, w_ref[2 * HEAD :, :])
        mean_square = jnp.mean(out * out, axis=1, keepdims=True)
        scale = jnp.where(head == 0, gain[0:1, :], gain[1:2, :])
        combined.append((a_ref[...] + out * lax.rsqrt(mean_square + EPSILON) * scale).astype(BF))
    send_ref[...] = (dot(combined[0], s0[...]) + dot(combined[1], s1[...])).astype(BF)
    own_ref[...] = dot(combined[0], o0[...]) + dot(combined[1], o1[...])


def tail_chunk(at, where, queries, attended, mine, theirs, gain, out_weight):
    columns = out_weight.shape[1] // 2
    whole = pl.BlockSpec((3 * HEAD, HEAD), lambda i, w: (0, 0))

    def token(row, mirror):
        return pl.BlockSpec((CHUNK, HEAD), lambda i, w: (row, 1 - w[0] if mirror else w[0]))

    def out_rows(mirror, send):
        return pl.BlockSpec(
            (HEAD, columns),
            lambda i, w: (1 - w[0] if mirror else w[0], 1 - w[1] if send else w[1]),
        )

    block = pl.BlockSpec((CHUNK, columns), lambda i, w: (0, 0))
    return pl.pallas_call(
        tail_body,
        out_shape=(
            jax.ShapeDtypeStruct((CHUNK, columns), BF),
            jax.ShapeDtypeStruct((CHUNK, columns), F32),
        ),
        grid_spec=pltpu.PrefetchScalarGridSpec(
            num_scalar_prefetch=1,
            grid=(1,),
            in_specs=[
                token(at, False),
                token(at, True),
                token(0, False),
                token(0, True),
                whole,
                whole,
                pl.BlockSpec((2, HEAD), lambda i, w: (0, 0)),
                out_rows(False, True),
                out_rows(True, True),
                out_rows(False, False),
                out_rows(True, False),
            ],
            out_specs=[block, block],
        ),
        compiler_params=pltpu.CompilerParams(vmem_limit_bytes=40 * MIB),
    )(
        where,
        queries,
        queries,
        attended,
        attended,
        mine,
        theirs,
        gain,
        out_weight,
        out_weight,
        out_weight,
        out_weight,
    )


def partner(value, flip):
    count = lax.axis_size("seq")
    return lax.ppermute(value, "seq", [(i, i ^ flip) for i in range(count)])


def over_planes(value):
    groups = [[p * PLANE + r for p in range(PLANES)] for r in range(PLANE)]
    return lax.all_to_all(value, "seq", 0, 0, tiled=True, axis_index_groups=groups)


def shards(
    queries,
    key_rows,
    value_rows,
    token_rates,
    gate_fast,
    lift_fast,
    down_fast,
    memory_gain,
    out_weight,
):
    queries, key_rows, value_rows, gate_fast, lift_fast, down_fast, out_weight = (
        pltpu.with_memory_space_constraint(x, pltpu.HBM)
        for x in (queries, key_rows, value_rows, gate_fast, lift_fast, down_fast, out_weight)
    )
    tokens_here = queries.shape[0]
    chunks = tokens_here // CHUNK
    seq = lax.axis_index("seq")
    core = (seq % 2).astype(jnp.int32)
    head = lax.axis_index("head").astype(jnp.int32)
    where = jnp.stack([core, head])
    mirrored = jnp.stack([1 - core, head])
    has_edge = jnp.where(seq > 0, 1, 0).astype(jnp.int32).reshape(1)

    fast = (gate_fast, lift_fast, down_fast)
    tokens = (key_rows, value_rows, token_rates)
    grads_send = head_grads(mirrored, *tokens, *fast, BF)
    grads_got = partner(grads_send, 1)
    grads_mine = head_grads(where, *tokens, *fast, F32)

    count = lax.axis_size("seq")
    along = [(i, i + 1) for i in range(count - 1)]
    edge_keys = lax.ppermute(key_rows, "seq", along)
    edge_values = lax.ppermute(value_rows, "seq", along)

    chip_sum = (grads_mine + grads_got.astype(F32)).astype(BF)
    slices = over_planes(chip_sum.reshape(PLANES, -1, HEAD))
    part = slices.astype(F32).sum(axis=0).astype(BF)
    other = partner(part, 2)
    part = (part.astype(F32) + other.astype(F32)).astype(BF)
    spread = jnp.broadcast_to(part[None], (PLANES, *part.shape))
    grads = over_planes(spread).reshape(3 * HEAD, HEAD)

    weights_mine = renewed_weights(where, grads, *fast)
    weights_theirs = partner(weights_mine, 1)

    head_pair = [(0, 1), (1, 0)]
    owns, arrivals = [], []
    after = ()
    for at in range(chunks):
        attended = attention_chunk(
            at, has_edge, queries, key_rows, value_rows, edge_keys, edge_values, after
        )
        send, own = tail_chunk(
            at, where, queries, attended, weights_mine, weights_theirs, memory_gain, out_weight
        )
        owns.append(own)
        arrivals.append(lax.ppermute(send, "head", head_pair))
        after = (send,)
    out = jnp.zeros((tokens_here, owns[0].shape[1]), BF)
    for at in range(chunks):
        rows = (owns[at] + arrivals[at].astype(F32)).astype(BF)
        out = lax.dynamic_update_slice(out, rows, (at * CHUNK, 0))
    return out


def solution(mesh):
    return jax.shard_map(
        shards,
        mesh=mesh,
        in_specs=(
            P("seq", "head"),
            P("seq", "head"),
            P("seq", "head"),
            P("head", "seq"),
            P("head", None, None),
            P("head", None, None),
            P("head", None, None),
            P("head", None),
            P("head", None),
        ),
        out_specs=P("seq", "head"),
        check_vma=False,
    )
```

```python
import jax
import jax.numpy as jnp
from jax import lax
from jax.experimental import pallas as pl
from jax.experimental.pallas import tpu as pltpu
from jax.sharding import PartitionSpec as P


HEAD = 512
WINDOW = 1024
NS_STEPS = 2
COEF_A = 3.4445
COEF_B = -4.775
COEF_C = 2.0315
EPSILON = 1e-06

CHUNK = 256
BF = jnp.bfloat16
F32 = jnp.float32
MIB = 1 << 20

PLANE = 4
PLANES = 16

ROW_BY_ROW = (((1,), (1,)), ((), ()))
COL_BY_COL = (((0,), (0,)), ((), ()))


def dot(a, b):
    return jnp.dot(a, b, preferred_element_type=F32)


def dot_on(a, b, dims):
    return lax.dot_general(a, b, dims, preferred_element_type=F32)


def any_spec():
    return pl.BlockSpec(memory_space=pl.ANY)


def sigmoid(x):
    return 0.5 * jnp.tanh(0.5 * x) + 0.5


def grads_body(where, k_ref, v_ref, rate_ref, gate_ref, lift_ref, down_ref, out_ref, acc, w16, back):
    step = pl.program_id(0)

    @pl.when(step == 0)
    def _():
        w16[:, :HEAD] = gate_ref[0].astype(BF)
        w16[:, HEAD : 2 * HEAD] = lift_ref[0].astype(BF)
        w16[:, 2 * HEAD :] = down_ref[0].astype(BF)

    keys = k_ref[...]
    rates = jnp.where(where[0] == 0, rate_ref[0:1, :], rate_ref[1:2, :])
    rate_col = jnp.broadcast_to(rates, (128, rates.shape[1])).T[:, :1]
    target = (-rate_col * v_ref[...].astype(F32)).astype(BF)
    gate_pre = dot(keys, w16[:, :HEAD])
    lift_pre = dot(keys, w16[:, HEAD : 2 * HEAD])
    back_hidden = dot_on(target, w16[:, 2 * HEAD :], ROW_BY_ROW)
    sig = sigmoid(gate_pre)
    activated = gate_pre * sig
    hidden = (activated * lift_pre).astype(BF)
    back[:, :HEAD] = (back_hidden * lift_pre * (sig + activated * (1.0 - sig))).astype(BF)
    back[:, HEAD:] = (back_hidden * activated).astype(BF)
    into = dot_on(keys, back[...], COL_BY_COL)
    down = dot_on(hidden, target, COL_BY_COL)

    @pl.when(step == 0)
    def _():
        acc[:, : 2 * HEAD] = into
        acc[:, 2 * HEAD :] = down

    @pl.when(step == pl.num_programs(0) - 1)
    def _():
        total_into = acc[:, : 2 * HEAD] + into
        total_down = acc[:, 2 * HEAD :] + down
        out_ref[:HEAD, :] = total_into[:, :HEAD].astype(out_ref.dtype)
        out_ref[HEAD : 2 * HEAD, :] = total_into[:, HEAD:].astype(out_ref.dtype)
        out_ref[2 * HEAD :, :] = total_down.astype(out_ref.dtype)


def head_grads(which, keys, values, rates, gate, lift, down, dtype):
    rows = keys.shape[0] // 2
    weight = pl.BlockSpec((1, HEAD, HEAD), lambda i, w: (w[0], 0, 0))
    token = pl.BlockSpec((rows, HEAD), lambda i, w: (i, w[0]))
    return pl.pallas_call(
        grads_body,
        out_shape=jax.ShapeDtypeStruct((3 * HEAD, HEAD), dtype),
        grid_spec=pltpu.PrefetchScalarGridSpec(
            num_scalar_prefetch=1,
            grid=(2,),
            in_specs=[
                token,
                token,
                pl.BlockSpec((2, rows), lambda i, w: (0, i)),
                weight,
                weight,
                weight,
            ],
            out_specs=pl.BlockSpec((3 * HEAD, HEAD), lambda i, w: (0, 0)),
            scratch_shapes=[
                pltpu.VMEM((HEAD, 3 * HEAD), F32),
                pltpu.VMEM((HEAD, 3 * HEAD), BF),
                pltpu.VMEM((rows, 2 * HEAD), BF),
            ],
        ),
        compiler_params=pltpu.CompilerParams(
            dimension_semantics=("arbitrary",), vmem_limit_bytes=40 * MIB
        ),
        name="head_grads",
    )(which, keys, values, rates, gate, lift, down)


def renew_body(where, g_ref, gate_ref, lift_ref, down_ref, out_ref, olds, sems):
    copies = [
        pltpu.make_async_copy(ref.at[where[0]], olds.at[i], sems.at[i])
        for i, ref in enumerate((gate_ref, lift_ref, down_ref))
    ]
    for copy in copies:
        copy.start()
    eye = (
        lax.broadcasted_iota(jnp.int32, (HEAD, HEAD), 0)
        == lax.broadcasted_iota(jnp.int32, (HEAD, HEAD), 1)
    ).astype(F32)
    iterates, grams = [], []
    for i in range(3):
        g = g_ref[i * HEAD : (i + 1) * HEAD, :]
        wide = g.astype(F32)
        gram = dot_on(g, g, COL_BY_COL)
        squares = jnp.sum(wide * wide, axis=0, keepdims=True)
        inverse = lax.rsqrt(jnp.sum(squares, axis=1, keepdims=True) + EPSILON)
        iterates.append((wide * inverse).astype(BF))
        grams.append(gram * (inverse * inverse))
    for sweep in range(NS_STEPS):
        polys = []
        for i in range(3):
            half = grams[i].astype(BF)
            square = dot(half, half)
            polys.append((COEF_A * eye + COEF_B * grams[i] + COEF_C * square).astype(BF))
        for i in range(3):
            iterates[i] = dot(iterates[i], polys[i]).astype(BF)
        if sweep + 1 < NS_STEPS:
            for i in range(3):
                grams[i] = dot_on(iterates[i], iterates[i], COL_BY_COL)
    for i in range(3):
        copies[i].wait()
        old = olds[i]
        change = old - iterates[i].astype(F32)
        old_square = jnp.sum(old * old, axis=0, keepdims=True)
        new_square = jnp.sum(change * change, axis=0, keepdims=True)
        out_ref[i * HEAD : (i + 1) * HEAD, :] = (
            change * jnp.sqrt(old_square / (new_square + EPSILON))
        ).astype(BF)


def renewed_weights(which, grads, gate, lift, down):
    whole = pl.BlockSpec((3 * HEAD, HEAD), lambda i, w: (0, 0))
    return pl.pallas_call(
        renew_body,
        out_shape=jax.ShapeDtypeStruct((3 * HEAD, HEAD), BF),
        grid_spec=pltpu.PrefetchScalarGridSpec(
            num_scalar_prefetch=1,
            grid=(1,),
            in_specs=[whole, any_spec(), any_spec(), any_spec()],
            out_specs=whole,
            scratch_shapes=[pltpu.VMEM((3, HEAD, HEAD), F32), pltpu.SemaphoreType.DMA((3,))],
        ),
        compiler_params=pltpu.CompilerParams(vmem_limit_bytes=48 * MIB),
        name="renewed_weights",
    )(which, grads, gate, lift, down)


def attention_chunk(at, has_edge, queries, keys, values, edge_keys, edge_values, after):
    blocks = WINDOW // CHUNK
    total = blocks + 1
    from_edge = blocks - at
    scale = HEAD ** (-0.5)

    def body(flag, q_ref, *refs):
        k_refs, v_refs, out_ref = refs[:total], refs[total : 2 * total], refs[-1]
        q = q_ref[...]
        row = lax.broadcasted_iota(jnp.int32, (CHUNK, CHUNK), 0)
        col = lax.broadcasted_iota(jnp.int32, (CHUNK, CHUNK), 1)
        scores = [dot_on(q, k_refs[j][...], ROW_BY_ROW) for j in range(total)]
        scores[0] = jnp.where(col > row, scores[0], -jnp.inf)
        scores[-1] = jnp.where(col <= row, scores[-1], -jnp.inf)
        edge_on = flag[0] > 0

        def rowmax(parts):
            best = parts[0]
            for part in parts[1:]:
                best = jnp.maximum(best, part)
            return jnp.max(best, axis=1, keepdims=True)

        own_max = rowmax(scores[from_edge:])
        both_max = jnp.maximum(own_max, rowmax(scores[:from_edge]))
        largest = jnp.where(edge_on, both_max, own_max)
        edge_largest = jnp.where(edge_on, both_max, jnp.inf)
        weights = [
            jnp.exp((scores[j] - (edge_largest if j < from_edge else largest)) * scale)
            for j in range(total)
        ]
        together = weights[0]
        for part in weights[1:]:
            together = together + part
        summed = jnp.sum(together, axis=1, keepdims=True)
        mixed = dot(weights[0].astype(BF), v_refs[0][...])
        for j in range(1, total):
            mixed = mixed + dot(weights[j].astype(BF), v_refs[j][...])
        out_ref[...] = mixed / summed

    def spec(row):
        return pl.BlockSpec((CHUNK, HEAD), lambda h, flag: (row, h))

    rows = [spec(at + j) for j in range(from_edge)] + [spec(j) for j in range(at + 1)]
    key_args = [edge_keys] * from_edge + [keys] * (at + 1)
    value_args = [edge_values] * from_edge + [values] * (at + 1)
    width = queries.shape[1]
    return pl.pallas_call(
        body,
        out_shape=jax.ShapeDtypeStruct((CHUNK, width), F32),
        grid_spec=pltpu.PrefetchScalarGridSpec(
            num_scalar_prefetch=1,
            grid=(width // HEAD,),
            in_specs=[spec(at)] + rows + rows + [any_spec()] * len(after),
            out_specs=pl.BlockSpec((CHUNK, HEAD), lambda h, flag: (0, h)),
        ),
        compiler_params=pltpu.CompilerParams(vmem_limit_bytes=32 * MIB),
    )(has_edge, queries, *key_args, *value_args, *after)


def tail_body(where, q0, q1, a0, a1, w0, w1, gain, s0, s1, o0, o1, send_ref, own_ref):
    combined = []
    for q_ref, a_ref, w_ref, head in ((q0, a0, w0, where[0]), (q1, a1, w1, 1 - where[0])):
        q = q_ref[...]
        gate = dot(q, w_ref[0:HEAD, :])
        lift = dot(q, w_ref[HEAD : 2 * HEAD, :])
        hidden = (gate * sigmoid(gate) * lift).astype(BF)
        out = dot(hidden, w_ref[2 * HEAD :, :])
        mean_square = jnp.mean(out * out, axis=1, keepdims=True)
        scale = jnp.where(head == 0, gain[0:1, :], gain[1:2, :])
        combined.append((a_ref[...] + out * lax.rsqrt(mean_square + EPSILON) * scale).astype(BF))
    send_ref[...] = (dot(combined[0], s0[...]) + dot(combined[1], s1[...])).astype(BF)
    own_ref[...] = dot(combined[0], o0[...]) + dot(combined[1], o1[...])


def tail_chunk(at, where, queries, attended, mine, theirs, gain, out_weight):
    columns = out_weight.shape[1] // 2
    whole = pl.BlockSpec((3 * HEAD, HEAD), lambda i, w: (0, 0))

    def token(row, mirror):
        return pl.BlockSpec((CHUNK, HEAD), lambda i, w: (row, 1 - w[0] if mirror else w[0]))

    def out_rows(mirror, send):
        return pl.BlockSpec(
            (HEAD, columns),
            lambda i, w: (1 - w[0] if mirror else w[0], 1 - w[1] if send else w[1]),
        )

    block = pl.BlockSpec((CHUNK, columns), lambda i, w: (0, 0))
    return pl.pallas_call(
        tail_body,
        out_shape=(
            jax.ShapeDtypeStruct((CHUNK, columns), BF),
            jax.ShapeDtypeStruct((CHUNK, columns), F32),
        ),
        grid_spec=pltpu.PrefetchScalarGridSpec(
            num_scalar_prefetch=1,
            grid=(1,),
            in_specs=[
                token(at, False),
                token(at, True),
                token(0, False),
                token(0, True),
                whole,
                whole,
                pl.BlockSpec((2, HEAD), lambda i, w: (0, 0)),
                out_rows(False, True),
                out_rows(True, True),
                out_rows(False, False),
                out_rows(True, False),
            ],
            out_specs=[block, block],
        ),
        compiler_params=pltpu.CompilerParams(vmem_limit_bytes=40 * MIB),
    )(
        where,
        queries,
        queries,
        attended,
        attended,
        mine,
        theirs,
        gain,
        out_weight,
        out_weight,
        out_weight,
        out_weight,
    )


def partner(value, flip):
    count = lax.axis_size("seq")
    return lax.ppermute(value, "seq", [(i, i ^ flip) for i in range(count)])


def over_planes(value):
    groups = [[p * PLANE + r for p in range(PLANES)] for r in range(PLANE)]
    return lax.all_to_all(value, "seq", 0, 0, tiled=True, axis_index_groups=groups)


def shards(
    queries,
    key_rows,
    value_rows,
    token_rates,
    gate_fast,
    lift_fast,
    down_fast,
    memory_gain,
    out_weight,
):
    queries, key_rows, value_rows, gate_fast, lift_fast, down_fast, out_weight = (
        pltpu.with_memory_space_constraint(x, pltpu.HBM)
        for x in (queries, key_rows, value_rows, gate_fast, lift_fast, down_fast, out_weight)
    )
    tokens_here = queries.shape[0]
    chunks = tokens_here // CHUNK
    seq = lax.axis_index("seq")
    core = (seq % 2).astype(jnp.int32)
    head = lax.axis_index("head").astype(jnp.int32)
    where = jnp.stack([core, head])
    mirrored = jnp.stack([1 - core, head])
    has_edge = jnp.where(seq > 0, 1, 0).astype(jnp.int32).reshape(1)

    fast = (gate_fast, lift_fast, down_fast)
    tokens = (key_rows, value_rows, token_rates)
    grads_send = head_grads(mirrored, *tokens, *fast, BF)
    grads_got = partner(grads_send, 1)
    grads_mine = head_grads(where, *tokens, *fast, F32)

    count = lax.axis_size("seq")
    along = [(i, i + 1) for i in range(count - 1)]
    edge_keys = lax.ppermute(key_rows, "seq", along)
    edge_values = lax.ppermute(value_rows, "seq", along)

    chip_sum = (grads_mine + grads_got.astype(F32)).astype(BF)
    slices = over_planes(chip_sum.reshape(PLANES, -1, HEAD))
    part = slices.astype(F32).sum(axis=0).astype(BF)
    other = partner(part, 2)
    part = (part.astype(F32) + other.astype(F32)).astype(BF)
    spread = jnp.broadcast_to(part[None], (PLANES, *part.shape))
    grads = over_planes(spread).reshape(3 * HEAD, HEAD)

    weights_mine = renewed_weights(where, grads, *fast)
    weights_theirs = partner(weights_mine, 1)

    head_pair = [(0, 1), (1, 0)]
    owns, arrivals = [], []
    after = ()
    for at in range(chunks):
        attended = attention_chunk(
            at, has_edge, queries, key_rows, value_rows, edge_keys, edge_values, after
        )
        send, own = tail_chunk(
            at, where, queries, attended, weights_mine, weights_theirs, memory_gain, out_weight
        )
        owns.append(own)
        arrivals.append(lax.ppermute(send, "head", head_pair))
        after = (send,)
    out = jnp.zeros((tokens_here, owns[0].shape[1]), BF)
    for at in range(chunks):
        rows = (owns[at] + arrivals[at].astype(F32)).astype(BF)
        out = lax.dynamic_update_slice(out, rows, (at * CHUNK, 0))
    return out


def solution(mesh):
    return jax.shard_map(
        shards,
        mesh=mesh,
        in_specs=(
            P("seq", "head"),
            P("seq", "head"),
            P("seq", "head"),
            P("head", "seq"),
            P("head", None, None),
            P("head", None, None),
            P("head", None, None),
            P("head", None),
            P("head", None),
        ),
        out_specs=P("seq", "head"),
        check_vma=False,
    )
```

```python
import jax
import jax.numpy as jnp
from jax import lax
from jax.experimental import pallas as pl
from jax.experimental.pallas import tpu as pltpu
from jax.sharding import PartitionSpec as P


HEAD = 512
WINDOW = 1024
NS_STEPS = 2
COEF_A = 3.4445
COEF_B = -4.775
COEF_C = 2.0315
EPSILON = 1e-06

CHUNK = 256
BF = jnp.bfloat16
F32 = jnp.float32
MIB = 1 << 20

PLANE = 4
PLANES = 16

ROW_BY_ROW = (((1,), (1,)), ((), ()))
COL_BY_COL = (((0,), (0,)), ((), ()))


def dot(a, b):
    return jnp.dot(a, b, preferred_element_type=F32)


def dot_on(a, b, dims):
    return lax.dot_general(a, b, dims, preferred_element_type=F32)


def any_spec():
    return pl.BlockSpec(memory_space=pl.ANY)


def sigmoid(x):
    return 0.5 * jnp.tanh(0.5 * x) + 0.5


def grads_body(where, k_ref, v_ref, rate_ref, gate_ref, lift_ref, down_ref, out_ref, acc, w16, back):
    step = pl.program_id(0)

    @pl.when(step == 0)
    def _():
        w16[:, :HEAD] = gate_ref[0].astype(BF)
        w16[:, HEAD : 2 * HEAD] = lift_ref[0].astype(BF)
        w16[:, 2 * HEAD :] = down_ref[0].astype(BF)

    keys = k_ref[...]
    rates = jnp.where(where[0] == 0, rate_ref[0:1, :], rate_ref[1:2, :])
    rate_col = jnp.broadcast_to(rates, (128, rates.shape[1])).T[:, :1]
    target = (-rate_col * v_ref[...].astype(F32)).astype(BF)
    gate_pre = dot(keys, w16[:, :HEAD])
    lift_pre = dot(keys, w16[:, HEAD : 2 * HEAD])
    back_hidden = dot_on(target, w16[:, 2 * HEAD :], ROW_BY_ROW)
    sig = sigmoid(gate_pre)
    activated = gate_pre * sig
    hidden = (activated * lift_pre).astype(BF)
    back[:, :HEAD] = (back_hidden * lift_pre * (sig + activated * (1.0 - sig))).astype(BF)
    back[:, HEAD:] = (back_hidden * activated).astype(BF)
    into = dot_on(keys, back[...], COL_BY_COL)
    down = dot_on(hidden, target, COL_BY_COL)

    @pl.when(step == 0)
    def _():
        acc[:, : 2 * HEAD] = into
        acc[:, 2 * HEAD :] = down

    @pl.when(step == pl.num_programs(0) - 1)
    def _():
        total_into = acc[:, : 2 * HEAD] + into
        total_down = acc[:, 2 * HEAD :] + down
        out_ref[:HEAD, :] = total_into[:, :HEAD].astype(out_ref.dtype)
        out_ref[HEAD : 2 * HEAD, :] = total_into[:, HEAD:].astype(out_ref.dtype)
        out_ref[2 * HEAD :, :] = total_down.astype(out_ref.dtype)


def head_grads(which, keys, values, rates, gate, lift, down, dtype):
    rows = keys.shape[0] // 2
    weight = pl.BlockSpec((1, HEAD, HEAD), lambda i, w: (w[0], 0, 0))
    token = pl.BlockSpec((rows, HEAD), lambda i, w: (i, w[0]))
    return pl.pallas_call(
        grads_body,
        out_shape=jax.ShapeDtypeStruct((3 * HEAD, HEAD), dtype),
        grid_spec=pltpu.PrefetchScalarGridSpec(
            num_scalar_prefetch=1,
            grid=(2,),
            in_specs=[
                token,
                token,
                pl.BlockSpec((2, rows), lambda i, w: (0, i)),
                weight,
                weight,
                weight,
            ],
            out_specs=pl.BlockSpec((3 * HEAD, HEAD), lambda i, w: (0, 0)),
            scratch_shapes=[
                pltpu.VMEM((HEAD, 3 * HEAD), F32),
                pltpu.VMEM((HEAD, 3 * HEAD), BF),
                pltpu.VMEM((rows, 2 * HEAD), BF),
            ],
        ),
        compiler_params=pltpu.CompilerParams(
            dimension_semantics=("arbitrary",), vmem_limit_bytes=40 * MIB
        ),
        name="head_grads",
    )(which, keys, values, rates, gate, lift, down)


def renew_body(where, g_ref, gate_ref, lift_ref, down_ref, out_ref, olds, sems):
    copies = [
        pltpu.make_async_copy(ref.at[where[0]], olds.at[i], sems.at[i])
        for i, ref in enumerate((gate_ref, lift_ref, down_ref))
    ]
    for copy in copies:
        copy.start()
    eye = (
        lax.broadcasted_iota(jnp.int32, (HEAD, HEAD), 0)
        == lax.broadcasted_iota(jnp.int32, (HEAD, HEAD), 1)
    ).astype(F32)
    iterates, grams = [], []
    for i in range(3):
        g = g_ref[i * HEAD : (i + 1) * HEAD, :]
        wide = g.astype(F32)
        gram = dot_on(g, g, COL_BY_COL)
        squares = jnp.sum(wide * wide, axis=0, keepdims=True)
        inverse = lax.rsqrt(jnp.sum(squares, axis=1, keepdims=True) + EPSILON)
        iterates.append((wide * inverse).astype(BF))
        grams.append(gram * (inverse * inverse))
    for sweep in range(NS_STEPS):
        polys = []
        for i in range(3):
            half = grams[i].astype(BF)
            square = dot(half, half)
            polys.append((COEF_A * eye + COEF_B * grams[i] + COEF_C * square).astype(BF))
        for i in range(3):
            iterates[i] = dot(iterates[i], polys[i]).astype(BF)
        if sweep + 1 < NS_STEPS:
            for i in range(3):
                grams[i] = dot_on(iterates[i], iterates[i], COL_BY_COL)
    for i in range(3):
        copies[i].wait()
        old = olds[i]
        change = old - iterates[i].astype(F32)
        old_square = jnp.sum(old * old, axis=0, keepdims=True)
        new_square = jnp.sum(change * change, axis=0, keepdims=True)
        out_ref[i * HEAD : (i + 1) * HEAD, :] = (
            change * jnp.sqrt(old_square / (new_square + EPSILON))
        ).astype(BF)


def renewed_weights(which, grads, gate, lift, down):
    whole = pl.BlockSpec((3 * HEAD, HEAD), lambda i, w: (0, 0))
    return pl.pallas_call(
        renew_body,
        out_shape=jax.ShapeDtypeStruct((3 * HEAD, HEAD), BF),
        grid_spec=pltpu.PrefetchScalarGridSpec(
            num_scalar_prefetch=1,
            grid=(1,),
            in_specs=[whole, any_spec(), any_spec(), any_spec()],
            out_specs=whole,
            scratch_shapes=[pltpu.VMEM((3, HEAD, HEAD), F32), pltpu.SemaphoreType.DMA((3,))],
        ),
        compiler_params=pltpu.CompilerParams(vmem_limit_bytes=48 * MIB),
        name="renewed_weights",
    )(which, grads, gate, lift, down)


SPAN = WINDOW + CHUNK


def scores_body(flag, q_ref, edge_ref, key_ref, out_ref, span, sems):
    head, at = pl.program_id(0), pl.program_id(1)
    heads = pl.num_programs(0)
    tokens = key_ref.shape[0]

    def copies(h):
        column = pl.ds(pl.multiple_of(h * HEAD, HEAD), HEAD)
        return (
            pltpu.make_async_copy(
                edge_ref.at[:, column], span.at[h, pl.ds(0, WINDOW)], sems.at[h, 0]
            ),
            pltpu.make_async_copy(
                key_ref.at[:, column], span.at[h, pl.ds(WINDOW, tokens)], sems.at[h, 1]
            ),
        )

    @pl.when((head == 0) & (at == 0))
    def _():
        for copy in copies(0):
            copy.start()

    @pl.when(at == 0)
    def _():
        for copy in copies(head):
            copy.wait()

    @pl.when((at == 0) & (head + 1 < heads))
    def _():
        for copy in copies(head + 1):
            copy.start()

    keys = span[head, pl.ds(pl.multiple_of(at * CHUNK, CHUNK), SPAN), :]
    scores = dot_on(q_ref[...], keys, ROW_BY_ROW)
    row = lax.broadcasted_iota(jnp.int32, scores.shape, 0)
    col = lax.broadcasted_iota(jnp.int32, scores.shape, 1)
    first = jnp.where(flag[0] > 0, 0, WINDOW - at * CHUNK)
    allowed = (col > row) & (col <= row + WINDOW) & (col >= first)
    scores = jnp.where(allowed, scores, -jnp.inf)
    largest = jnp.max(scores, axis=1, keepdims=True)
    exponent = jnp.exp((scores - largest) * (HEAD ** (-0.5)))
    summed = jnp.sum(exponent, axis=1, keepdims=True)
    out_ref[...] = (exponent * (1.0 / summed)).astype(BF)


def probabilities(has_edge, queries, edge_keys, keys):
    tokens, width = queries.shape
    heads = width // HEAD
    return pl.pallas_call(
        scores_body,
        out_shape=jax.ShapeDtypeStruct((tokens, heads * SPAN), BF),
        grid_spec=pltpu.PrefetchScalarGridSpec(
            num_scalar_prefetch=1,
            grid=(heads, tokens // CHUNK),
            in_specs=[
                pl.BlockSpec((CHUNK, HEAD), lambda h, i, flag: (i, h)),
                any_spec(),
                any_spec(),
            ],
            out_specs=pl.BlockSpec((CHUNK, SPAN), lambda h, i, flag: (i, h)),
            scratch_shapes=[
                pltpu.VMEM((heads, WINDOW + tokens, HEAD), BF),
                pltpu.SemaphoreType.DMA((heads, 2)),
            ],
        ),
        compiler_params=pltpu.CompilerParams(
            dimension_semantics=("arbitrary", "arbitrary"), vmem_limit_bytes=32 * MIB
        ),
        name="probabilities",
    )(has_edge, queries, edge_keys, keys)


PIECE = 2 * CHUNK


def combined_piece(at, mirror, where, queries, probability, weights, gain, edge_values, values):
    from_edge = WINDOW - at * PIECE
    from_own = (at + 1) * PIECE

    def head_of(w):
        return 1 - w[0] if mirror else w[0]

    def body(w, q_ref, p_ref, w_ref, gain_ref, edge_ref, value_ref, out_ref, span, sems):
        head = head_of(w)
        column = pl.ds(pl.multiple_of(head * HEAD, HEAD), HEAD)
        copies = (
            pltpu.make_async_copy(
                edge_ref.at[pl.ds(at * PIECE, from_edge), column],
                span.at[pl.ds(0, from_edge)],
                sems.at[0],
            ),
            pltpu.make_async_copy(
                value_ref.at[pl.ds(0, from_own), column],
                span.at[pl.ds(from_edge, from_own)],
                sems.at[1],
            ),
        )
        for copy in copies:
            copy.start()
        q = q_ref[...]
        gate = dot(q, w_ref[0:HEAD, :])
        lift = dot(q, w_ref[HEAD : 2 * HEAD, :])
        hidden = (gate * sigmoid(gate) * lift).astype(BF)
        out = dot(hidden, w_ref[2 * HEAD :, :])
        mean_square = jnp.mean(out * out, axis=1, keepdims=True)
        scale = jnp.where(head == 0, gain_ref[0:1, :], gain_ref[1:2, :])
        normed = out * lax.rsqrt(mean_square + EPSILON) * scale
        for copy in copies:
            copy.wait()
        for part in range(PIECE // CHUNK):
            rows = slice(part * CHUNK, (part + 1) * CHUNK)
            attended = dot(p_ref[rows, :], span[part * CHUNK : part * CHUNK + SPAN, :])
            out_ref[rows, :] = (attended + normed[rows, :]).astype(BF)

    return pl.pallas_call(
        body,
        out_shape=jax.ShapeDtypeStruct((PIECE, HEAD), BF),
        grid_spec=pltpu.PrefetchScalarGridSpec(
            num_scalar_prefetch=1,
            grid=(1,),
            in_specs=[
                pl.BlockSpec((PIECE, HEAD), lambda i, w: (at, head_of(w))),
                pl.BlockSpec((PIECE, SPAN), lambda i, w: (at, head_of(w))),
                pl.BlockSpec((3 * HEAD, HEAD), lambda i, w: (0, 0)),
                pl.BlockSpec((2, HEAD), lambda i, w: (0, 0)),
                any_spec(),
                any_spec(),
            ],
            out_specs=pl.BlockSpec((PIECE, HEAD), lambda i, w: (0, 0)),
            scratch_shapes=[
                pltpu.VMEM((WINDOW + PIECE, HEAD), BF),
                pltpu.SemaphoreType.DMA((2,)),
            ],
        ),
        compiler_params=pltpu.CompilerParams(vmem_limit_bytes=32 * MIB),
    )(where, queries, probability, weights, gain, edge_values, values)


def project_piece(where, combined, first_arrived, out_weight, other_weight):
    columns = out_weight.shape[1] // 2
    step = columns // 2

    def body(w, a_ref, b_ref, c_ref, wa_ref, wb_ref, wc_ref, out_ref):
        out_ref[...] = (
            dot(a_ref[...], wa_ref[...]) + dot(b_ref[...], wb_ref[...]) + dot(c_ref[...], wc_ref[...])
        )

    rows = pl.BlockSpec((PIECE, HEAD), lambda i, w: (0, 0))
    return pl.pallas_call(
        body,
        out_shape=jax.ShapeDtypeStruct((PIECE, columns), F32),
        grid_spec=pltpu.PrefetchScalarGridSpec(
            num_scalar_prefetch=1,
            grid=(2,),
            in_specs=[
                rows,
                rows,
                rows,
                pl.BlockSpec((HEAD, step), lambda i, w: (w[0], 2 * w[1] + i)),
                pl.BlockSpec((HEAD, step), lambda i, w: (1 - w[0], 2 * w[1] + i)),
                pl.BlockSpec((HEAD, step), lambda i, w: (w[0], i)),
            ],
            out_specs=pl.BlockSpec((PIECE, step), lambda i, w: (0, i)),
        ),
        compiler_params=pltpu.CompilerParams(vmem_limit_bytes=32 * MIB),
        name="project",
    )(where, *combined, first_arrived, out_weight, out_weight, other_weight)


def finish_piece(at, tokens, where, partial, last_arrived, other_weight, before):
    columns = partial.shape[1]
    step = columns // 2

    def body(w, acc_ref, a_ref, wa_ref, *refs):
        refs[-1][...] = (acc_ref[...] + dot(a_ref[...], wa_ref[...])).astype(BF)

    held = () if before is None else (before,)
    return pl.pallas_call(
        body,
        out_shape=jax.ShapeDtypeStruct((tokens, columns), BF),
        grid_spec=pltpu.PrefetchScalarGridSpec(
            num_scalar_prefetch=1,
            grid=(2,),
            in_specs=[
                pl.BlockSpec((PIECE, step), lambda i, w: (0, i)),
                pl.BlockSpec((PIECE, HEAD), lambda i, w: (0, 0)),
                pl.BlockSpec((HEAD, step), lambda i, w: (1 - w[0], i)),
            ]
            + [any_spec()] * len(held),
            out_specs=pl.BlockSpec((PIECE, step), lambda i, w: (at, i)),
        ),
        compiler_params=pltpu.CompilerParams(vmem_limit_bytes=32 * MIB),
        input_output_aliases={4: 0} if held else {},
    )(where, partial, last_arrived, other_weight, *held)


def partner(value, flip):
    count = lax.axis_size("seq")
    return lax.ppermute(value, "seq", [(i, i ^ flip) for i in range(count)])


def over_planes(value):
    groups = [[p * PLANE + r for p in range(PLANES)] for r in range(PLANE)]
    return lax.all_to_all(value, "seq", 0, 0, tiled=True, axis_index_groups=groups)


def shards(
    queries,
    key_rows,
    value_rows,
    token_rates,
    gate_fast,
    lift_fast,
    down_fast,
    memory_gain,
    out_weight,
):
    raw_out_weight = out_weight
    queries, key_rows, value_rows, token_rates, gate_fast, lift_fast, down_fast, out_weight = (
        pltpu.with_memory_space_constraint(x, pltpu.HBM)
        for x in (
            queries,
            key_rows,
            value_rows,
            token_rates,
            gate_fast,
            lift_fast,
            down_fast,
            out_weight,
        )
    )
    tokens_here = queries.shape[0]
    seq = lax.axis_index("seq")
    core = (seq % 2).astype(jnp.int32)
    head = lax.axis_index("head").astype(jnp.int32)
    where = jnp.stack([core, head])
    mirrored = jnp.stack([1 - core, head])
    has_edge = jnp.where(seq > 0, 1, 0).astype(jnp.int32).reshape(1)

    fast = (gate_fast, lift_fast, down_fast)
    tokens = (key_rows, value_rows, token_rates)
    grads_send = head_grads(mirrored, *tokens, *fast, BF)
    grads_got = partner(grads_send, 1)
    grads_mine = head_grads(where, *tokens, *fast, F32)

    count = lax.axis_size("seq")
    along = [(i, i + 1) for i in range(count - 1)]
    edge_keys = lax.ppermute(key_rows, "seq", along)
    edge_values = lax.ppermute(value_rows, "seq", along)

    chip_sum = (grads_mine + grads_got.astype(F32)).astype(BF)
    slices = over_planes(chip_sum.reshape(PLANES, -1, HEAD))
    part = slices.astype(F32).sum(axis=0).astype(BF)
    other = partner(part, 2)
    part = (part.astype(F32) + other.astype(F32)).astype(BF)
    spread = jnp.broadcast_to(part[None], (PLANES, *part.shape))
    grads = over_planes(spread).reshape(3 * HEAD, HEAD)

    weights_mine = renewed_weights(where, grads, *fast)
    weights_theirs = partner(weights_mine, 1)

    columns = out_weight.shape[1] // 2
    pairs = [
        (group * count + i, (1 - group) * count + (i ^ 2)) for group in range(2) for i in range(count)
    ]
    other_weight = lax.ppermute(
        lax.dynamic_slice(
            raw_out_weight, (0, (1 - head) * columns), (out_weight.shape[0], columns)
        ),
        ("head", "seq"),
        pairs,
    )

    probability = probabilities(has_edge, queries, edge_keys, key_rows)

    pieces = tokens_here // PIECE
    head_pair = [(0, 1), (1, 0)]
    made, arrived = {}, {}
    for mirror, weights in ((False, weights_mine), (True, weights_theirs)):
        for at in range(pieces):
            piece = combined_piece(
                at,
                mirror,
                where,
                queries,
                probability,
                weights,
                memory_gain,
                edge_values,
                value_rows,
            )
            made[mirror, at] = piece
            arrived[mirror, at] = lax.ppermute(piece, "head", head_pair)
    out = None
    for at in range(pieces):
        partial = project_piece(
            where,
            (made[False, at], made[True, at]),
            arrived[False, at],
            out_weight,
            other_weight,
        )
        out = finish_piece(
            at, tokens_here, where, partial, arrived[True, at], other_weight, out
        )
    return out


def solution(mesh):
    return jax.shard_map(
        shards,
        mesh=mesh,
        in_specs=(
            P("seq", "head"),
            P("seq", "head"),
            P("seq", "head"),
            P("head", "seq"),
            P("head", None, None),
            P("head", None, None),
            P("head", None, None),
            P("head", None),
            P("head", None),
        ),
        out_specs=P("seq", "head"),
        check_vma=False,
    )
```

```python
import jax
import jax.numpy as jnp
from jax import lax
from jax.experimental import pallas as pl
from jax.experimental.pallas import tpu as pltpu
from jax.sharding import PartitionSpec as P


HEAD = 512
WINDOW = 1024
NS_STEPS = 2
COEF_A = 3.4445
COEF_B = -4.775
COEF_C = 2.0315
EPSILON = 1e-06

CHUNK = 256
BF = jnp.bfloat16
F32 = jnp.float32
MIB = 1 << 20

PLANE = 4
PLANES = 16

ROW_BY_ROW = (((1,), (1,)), ((), ()))
COL_BY_COL = (((0,), (0,)), ((), ()))


def dot(a, b):
    return jnp.dot(a, b, preferred_element_type=F32)


def dot_on(a, b, dims):
    return lax.dot_general(a, b, dims, preferred_element_type=F32)


def any_spec():
    return pl.BlockSpec(memory_space=pl.ANY)


def sigmoid(x):
    return 0.5 * jnp.tanh(0.5 * x) + 0.5


def vmem_spec():
    return pl.BlockSpec(memory_space=pltpu.VMEM)


def grads_body(where, k_hbm, v_hbm, rate_ref, gate_hbm, lift_hbm, down_hbm, out_ref, k_ref, v_ref, fast, sems):
    head = where[0]
    tokens = k_ref.shape[0]
    half = tokens // 2
    column = pl.ds(pl.multiple_of(head * HEAD, HEAD), HEAD)
    moves = []

    def fetch(source, target):
        copy = pltpu.make_async_copy(source, target, sems.at[len(moves)])
        copy.start()
        moves.append(copy)
        return copy

    def rows_of(n):
        return pl.ds(n * half, half)

    waits = {
        "k0": fetch(k_hbm.at[rows_of(0), column], k_ref.at[rows_of(0)]),
        "gate": fetch(gate_hbm.at[head], fast.at[0]),
        "lift": fetch(lift_hbm.at[head], fast.at[1]),
        "v0": fetch(v_hbm.at[rows_of(0), column], v_ref.at[rows_of(0)]),
        "down": fetch(down_hbm.at[head], fast.at[2]),
        "k1": fetch(k_hbm.at[rows_of(1), column], k_ref.at[rows_of(1)]),
        "v1": fetch(v_hbm.at[rows_of(1), column], v_ref.at[rows_of(1)]),
    }
    rates = jnp.where(head == 0, rate_ref[0:1, :], rate_ref[1:2, :])
    rate_col = jnp.broadcast_to(rates, (128, tokens)).T[:, :1]
    waits["k0"].wait()
    waits["gate"].wait()
    gate = fast[0].astype(BF)
    into_gate = into_lift = down_sum = None
    lift = down = None
    for n in range(2):
        rows = slice(n * half, (n + 1) * half)
        if n:
            waits["k1"].wait()
        keys = k_ref[rows, :]
        gate_pre = dot(keys, gate)
        sig = sigmoid(gate_pre)
        activated = gate_pre * sig
        slope = sig + activated * (1.0 - sig)
        if lift is None:
            waits["lift"].wait()
            lift = fast[1].astype(BF)
        lift_pre = dot(keys, lift)
        hidden = (activated * lift_pre).astype(BF)
        slope = lift_pre * slope
        waits["v1" if n else "v0"].wait()
        target = (-rate_col[rows, :] * v_ref[rows, :].astype(F32)).astype(BF)
        if down is None:
            waits["down"].wait()
            down = fast[2].astype(BF)
        back_hidden = dot_on(target, down, ROW_BY_ROW)
        back_gate = (back_hidden * slope).astype(BF)
        back_lift = (back_hidden * activated).astype(BF)
        parts = (
            dot_on(keys, back_gate, COL_BY_COL),
            dot_on(keys, back_lift, COL_BY_COL),
            dot_on(hidden, target, COL_BY_COL),
        )
        if n == 0:
            into_gate, into_lift, down_sum = parts
        else:
            for m, (first, second) in enumerate(zip((into_gate, into_lift, down_sum), parts)):
                out_ref[m * HEAD : (m + 1) * HEAD, :] = (first + second).astype(out_ref.dtype)


def head_grads(which, keys, values, rates, gate, lift, down, dtype):
    tokens = keys.shape[0]
    return pl.pallas_call(
        grads_body,
        out_shape=jax.ShapeDtypeStruct((3 * HEAD, HEAD), dtype),
        grid_spec=pltpu.PrefetchScalarGridSpec(
            num_scalar_prefetch=1,
            grid=(1,),
            in_specs=[
                any_spec(),
                any_spec(),
                pl.BlockSpec((2, tokens), lambda i, w: (0, 0)),
                any_spec(),
                any_spec(),
                any_spec(),
            ],
            out_specs=vmem_spec(),
            scratch_shapes=[
                pltpu.VMEM((tokens, HEAD), BF),
                pltpu.VMEM((tokens, HEAD), BF),
                pltpu.VMEM((3, HEAD, HEAD), F32),
                pltpu.SemaphoreType.DMA((7,)),
            ],
        ),
        compiler_params=pltpu.CompilerParams(vmem_limit_bytes=30 * MIB),
        name="head_grads",
    )(which, keys, values, rates, gate, lift, down)


def renew_body(where, g_ref, gate_ref, lift_ref, down_ref, out_ref, olds, sems):
    copies = [
        pltpu.make_async_copy(ref.at[where[0]], olds.at[i], sems.at[i])
        for i, ref in enumerate((gate_ref, lift_ref, down_ref))
    ]
    for copy in copies:
        copy.start()
    eye = (
        lax.broadcasted_iota(jnp.int32, (HEAD, HEAD), 0)
        == lax.broadcasted_iota(jnp.int32, (HEAD, HEAD), 1)
    ).astype(F32)
    iterates, grams = [], []
    for i in range(3):
        g = g_ref[i * HEAD : (i + 1) * HEAD, :]
        wide = g.astype(F32)
        gram = dot_on(g, g, COL_BY_COL)
        squares = jnp.sum(wide * wide, axis=0, keepdims=True)
        inverse = lax.rsqrt(jnp.sum(squares, axis=1, keepdims=True) + EPSILON)
        iterates.append((wide * inverse).astype(BF))
        grams.append(gram * (inverse * inverse))
    for sweep in range(NS_STEPS):
        polys = []
        for i in range(3):
            half = grams[i].astype(BF)
            square = dot(half, half)
            polys.append((COEF_A * eye + COEF_B * grams[i] + COEF_C * square).astype(BF))
        for i in range(3):
            iterates[i] = dot(iterates[i], polys[i]).astype(BF)
        if sweep + 1 < NS_STEPS:
            for i in range(3):
                grams[i] = dot_on(iterates[i], iterates[i], COL_BY_COL)
    for i in range(3):
        copies[i].wait()
        old = olds[i]
        change = old - iterates[i].astype(F32)
        old_square = jnp.sum(old * old, axis=0, keepdims=True)
        new_square = jnp.sum(change * change, axis=0, keepdims=True)
        out_ref[i * HEAD : (i + 1) * HEAD, :] = (
            change * jnp.sqrt(old_square / (new_square + EPSILON))
        ).astype(BF)


def renewed_weights(which, grads, gate, lift, down):
    return pl.pallas_call(
        renew_body,
        out_shape=jax.ShapeDtypeStruct((3 * HEAD, HEAD), BF),
        grid_spec=pltpu.PrefetchScalarGridSpec(
            num_scalar_prefetch=1,
            grid=(1,),
            in_specs=[vmem_spec(), any_spec(), any_spec(), any_spec()],
            out_specs=vmem_spec(),
            scratch_shapes=[pltpu.VMEM((3, HEAD, HEAD), F32), pltpu.SemaphoreType.DMA((3,))],
        ),
        compiler_params=pltpu.CompilerParams(vmem_limit_bytes=24 * MIB),
        name="renewed_weights",
    )(which, grads, gate, lift, down)


SPAN = WINDOW + CHUNK


def scores_body(flag, q_ref, edge_ref, key_ref, out_ref, span, sems):
    head, at = pl.program_id(0), pl.program_id(1)
    heads = pl.num_programs(0)
    tokens = key_ref.shape[0]

    def copies(h):
        column = pl.ds(pl.multiple_of(h * HEAD, HEAD), HEAD)
        return (
            pltpu.make_async_copy(
                edge_ref.at[:, column], span.at[h, pl.ds(0, WINDOW)], sems.at[h, 0]
            ),
            pltpu.make_async_copy(
                key_ref.at[:, column], span.at[h, pl.ds(WINDOW, tokens)], sems.at[h, 1]
            ),
        )

    @pl.when((head == 0) & (at == 0))
    def _():
        for copy in copies(0):
            copy.start()

    @pl.when(at == 0)
    def _():
        for copy in copies(head):
            copy.wait()

    @pl.when((at == 0) & (head + 1 < heads))
    def _():
        for copy in copies(head + 1):
            copy.start()

    keys = span[head, pl.ds(pl.multiple_of(at * CHUNK, CHUNK), SPAN), :]
    scores = dot_on(q_ref[...], keys, ROW_BY_ROW)
    row = lax.broadcasted_iota(jnp.int32, scores.shape, 0)
    col = lax.broadcasted_iota(jnp.int32, scores.shape, 1)
    first = jnp.where(flag[0] > 0, 0, WINDOW - at * CHUNK)
    allowed = (col > row) & (col <= row + WINDOW) & (col >= first)
    scores = jnp.where(allowed, scores, -jnp.inf)
    largest = jnp.max(scores, axis=1, keepdims=True)
    exponent = jnp.exp((scores - largest) * (HEAD ** (-0.5)))
    summed = jnp.sum(exponent, axis=1, keepdims=True)
    out_ref[...] = (exponent * (1.0 / summed)).astype(BF)


def probabilities(has_edge, queries, edge_keys, keys):
    tokens, width = queries.shape
    heads = width // HEAD
    return pl.pallas_call(
        scores_body,
        out_shape=jax.ShapeDtypeStruct((tokens, heads * SPAN), BF),
        grid_spec=pltpu.PrefetchScalarGridSpec(
            num_scalar_prefetch=1,
            grid=(heads, tokens // CHUNK),
            in_specs=[
                pl.BlockSpec((CHUNK, HEAD), lambda h, i, flag: (i, h)),
                any_spec(),
                any_spec(),
            ],
            out_specs=pl.BlockSpec((CHUNK, SPAN), lambda h, i, flag: (i, h)),
            scratch_shapes=[
                pltpu.VMEM((heads, WINDOW + tokens, HEAD), BF),
                pltpu.SemaphoreType.DMA((heads, 2)),
            ],
        ),
        compiler_params=pltpu.CompilerParams(
            dimension_semantics=("arbitrary", "arbitrary"), vmem_limit_bytes=24 * MIB
        ),
        name="probabilities",
    )(has_edge, queries, edge_keys, keys)


PIECE = 2 * CHUNK


def combined_piece(at, mirror, where, queries, probability, weights, gain, edges, values, after):
    from_edge = sum(edge.shape[0] for edge in edges)
    from_own = (at + 1) * PIECE

    def head_of(w):
        return 1 - w[0] if mirror else w[0]

    def body(w, q_hbm, p_hbm, w_ref, gain_ref, value_hbm, *refs):
        edge_hbm, (out_ref, q_ref, p_ref, span, sems) = refs[: len(edges)], refs[-5:]
        head = head_of(w)
        column = pl.ds(pl.multiple_of(head * HEAD, HEAD), HEAD)
        chances = pl.ds(pl.multiple_of(head * SPAN, SPAN), SPAN)
        rows = pl.ds(at * PIECE, PIECE)
        moves = [
            (q_hbm.at[rows, column], q_ref),
            (p_hbm.at[rows, chances], p_ref),
            (value_hbm.at[pl.ds(0, from_own), column], span.at[pl.ds(from_edge, from_own)]),
        ]
        start = 0
        for edge in edge_hbm:
            count = edge.shape[0]
            moves.append((edge.at[:, column], span.at[pl.ds(start, count)]))
            start += count
        copies = [
            pltpu.make_async_copy(source, target, sems.at[n])
            for n, (source, target) in enumerate(moves)
        ]
        for copy in copies:
            copy.start()
        copies[0].wait()
        q = q_ref[...]
        gate = dot(q, w_ref[0:HEAD, :])
        lift = dot(q, w_ref[HEAD : 2 * HEAD, :])
        hidden = (gate * sigmoid(gate) * lift).astype(BF)
        out = dot(hidden, w_ref[2 * HEAD :, :])
        mean_square = jnp.mean(out * out, axis=1, keepdims=True)
        scale = jnp.where(head == 0, gain_ref[0:1, :], gain_ref[1:2, :])
        normed = out * lax.rsqrt(mean_square + EPSILON) * scale
        for copy in copies[1:]:
            copy.wait()
        for part in range(PIECE // CHUNK):
            rows = slice(part * CHUNK, (part + 1) * CHUNK)
            attended = dot(p_ref[rows, :], span[part * CHUNK : part * CHUNK + SPAN, :])
            out_ref[rows, :] = (attended + normed[rows, :]).astype(BF)

    return pl.pallas_call(
        body,
        out_shape=jax.ShapeDtypeStruct((PIECE, HEAD), BF),
        grid_spec=pltpu.PrefetchScalarGridSpec(
            num_scalar_prefetch=1,
            grid=(1,),
            in_specs=[any_spec(), any_spec(), vmem_spec(), vmem_spec(), any_spec()]
            + [any_spec()] * (len(edges) + len(after)),
            out_specs=vmem_spec(),
            scratch_shapes=[
                pltpu.VMEM((PIECE, HEAD), BF),
                pltpu.VMEM((PIECE, SPAN), BF),
                pltpu.VMEM((WINDOW + PIECE, HEAD), BF),
                pltpu.SemaphoreType.DMA((3 + len(edges),)),
            ],
        ),
        compiler_params=pltpu.CompilerParams(vmem_limit_bytes=16 * MIB),
    )(where, queries, probability, weights, gain, values, *edges, *after)


def project_piece(where, combined, first_arrived, out_weight, other_weight):
    columns = out_weight.shape[1] // 2
    step = columns // 2

    def body(w, a_ref, b_ref, c_ref, wa_ref, wb_ref, wc_ref, out_ref):
        out_ref[...] = (
            dot(a_ref[...], wa_ref[...]) + dot(b_ref[...], wb_ref[...]) + dot(c_ref[...], wc_ref[...])
        )

    rows = pl.BlockSpec((PIECE, HEAD), lambda i, w: (0, 0))
    return pl.pallas_call(
        body,
        out_shape=jax.ShapeDtypeStruct((PIECE, columns), F32),
        grid_spec=pltpu.PrefetchScalarGridSpec(
            num_scalar_prefetch=1,
            grid=(2,),
            in_specs=[
                rows,
                rows,
                rows,
                pl.BlockSpec((HEAD, step), lambda i, w: (w[0], 2 * w[1] + i)),
                pl.BlockSpec((HEAD, step), lambda i, w: (1 - w[0], 2 * w[1] + i)),
                pl.BlockSpec((HEAD, step), lambda i, w: (w[0], i)),
            ],
            out_specs=pl.BlockSpec((PIECE, step), lambda i, w: (0, i)),
        ),
        compiler_params=pltpu.CompilerParams(vmem_limit_bytes=16 * MIB),
        name="project",
    )(where, *combined, first_arrived, out_weight, out_weight, other_weight)


def finish_piece(at, tokens, where, partial, last_arrived, other_weight, before):
    columns = partial.shape[1]
    step = columns // 2

    def body(w, acc_ref, a_ref, wa_ref, *refs):
        here = pl.ds(pl.multiple_of(pl.program_id(0) * step, step), step)
        rows = pl.ds(pl.multiple_of((1 - w[0]) * HEAD, HEAD), HEAD)
        refs[-1][...] = (acc_ref[:, here] + dot(a_ref[...], wa_ref[rows, here])).astype(BF)

    held = () if before is None else (before,)
    return pl.pallas_call(
        body,
        out_shape=jax.ShapeDtypeStruct((tokens, columns), BF),
        grid_spec=pltpu.PrefetchScalarGridSpec(
            num_scalar_prefetch=1,
            grid=(2,),
            in_specs=[vmem_spec(), vmem_spec(), vmem_spec()] + [any_spec()] * len(held),
            out_specs=pl.BlockSpec((PIECE, step), lambda i, w: (at, i)),
        ),
        compiler_params=pltpu.CompilerParams(vmem_limit_bytes=12 * MIB),
        input_output_aliases={4: 0} if held else {},
    )(where, partial, last_arrived, other_weight, *held)


def partner(value, flip):
    count = lax.axis_size("seq")
    return lax.ppermute(value, "seq", [(i, i ^ flip) for i in range(count)])


def over_planes(value):
    groups = [[p * PLANE + r for p in range(PLANES)] for r in range(PLANE)]
    return lax.all_to_all(value, "seq", 0, 0, tiled=True, axis_index_groups=groups)


def shards(
    queries,
    key_rows,
    value_rows,
    token_rates,
    gate_fast,
    lift_fast,
    down_fast,
    memory_gain,
    out_weight,
):
    raw_out_weight, raw_values = out_weight, value_rows
    queries, key_rows, value_rows, token_rates, gate_fast, lift_fast, down_fast, out_weight = (
        pltpu.with_memory_space_constraint(x, pltpu.HBM)
        for x in (
            queries,
            key_rows,
            value_rows,
            token_rates,
            gate_fast,
            lift_fast,
            down_fast,
            out_weight,
        )
    )
    tokens_here = queries.shape[0]
    seq = lax.axis_index("seq")
    core = (seq % 2).astype(jnp.int32)
    head = lax.axis_index("head").astype(jnp.int32)
    where = jnp.stack([core, head])
    mirrored = jnp.stack([1 - core, head])
    has_edge = jnp.where(seq > 0, 1, 0).astype(jnp.int32).reshape(1)

    fast = (gate_fast, lift_fast, down_fast)
    tokens = (key_rows, value_rows, token_rates)
    grads_send = head_grads(mirrored, *tokens, *fast, BF)
    grads_got = partner(grads_send, 1)
    grads_mine = head_grads(where, *tokens, *fast, F32)

    count = lax.axis_size("seq")
    along = [(i, i + 1) for i in range(count - 1)]
    edge_keys = lax.ppermute(key_rows, "seq", along)
    edge_late = lax.ppermute(raw_values[PIECE:], "seq", along)
    edge_early = lax.ppermute(raw_values[:PIECE], "seq", along)

    chip_sum = (grads_mine + grads_got.astype(F32)).astype(BF)
    slices = over_planes(chip_sum.reshape(PLANES, -1, HEAD))
    part = slices.astype(F32).sum(axis=0).astype(BF)
    other = partner(part, 2)
    part = (part.astype(F32) + other.astype(F32)).astype(BF)
    spread = jnp.broadcast_to(part[None], (PLANES, *part.shape))
    grads = over_planes(spread).reshape(3 * HEAD, HEAD)

    weights_mine = renewed_weights(where, grads, *fast)
    weights_theirs = partner(weights_mine, 1)

    columns = out_weight.shape[1] // 2
    pairs = [
        (group * count + i, (1 - group) * count + (i ^ 2)) for group in range(2) for i in range(count)
    ]
    other_weight = lax.ppermute(
        lax.dynamic_slice(
            raw_out_weight, (0, (1 - head) * columns), (out_weight.shape[0], columns)
        ),
        ("head", "seq"),
        pairs,
    )

    probability = pltpu.with_memory_space_constraint(
        probabilities(has_edge, queries, edge_keys, key_rows), pltpu.HBM
    )

    pieces = tokens_here // PIECE
    head_pair = [(0, 1), (1, 0)]
    made, arrived, after = {}, {}, ()
    for at in reversed(range(pieces)):
        edges = (edge_late,) if at else (edge_early, edge_late)
        for mirror, weights in ((False, weights_mine), (True, weights_theirs)):
            piece = combined_piece(
                at, mirror, where, queries, probability, weights, memory_gain, edges, value_rows, after
            )
            made[mirror, at], after = piece, (piece,)
            arrived[mirror, at] = lax.ppermute(piece, "head", head_pair)
    out = None
    for at in reversed(range(pieces)):
        partial = project_piece(
            where,
            (made[False, at], made[True, at]),
            arrived[False, at],
            out_weight,
            other_weight,
        )
        out = finish_piece(at, tokens_here, where, partial, arrived[True, at], other_weight, out)
    return out


def solution(mesh):
    return jax.shard_map(
        shards,
        mesh=mesh,
        in_specs=(
            P("seq", "head"),
            P("seq", "head"),
            P("seq", "head"),
            P("head", "seq"),
            P("head", None, None),
            P("head", None, None),
            P("head", None, None),
            P("head", None),
            P("head", None),
        ),
        out_specs=P("seq", "head"),
        check_vma=False,
    )
```

```python
import jax
import jax.numpy as jnp
from jax import lax
from jax.experimental import pallas as pl
from jax.experimental.pallas import tpu as pltpu
from jax.sharding import PartitionSpec as P


HEAD = 512
WINDOW = 1024
NS_STEPS = 2
COEF_A = 3.4445
COEF_B = -4.775
COEF_C = 2.0315
EPSILON = 1e-06

CHUNK = 256
BF = jnp.bfloat16
F32 = jnp.float32
MIB = 1 << 20

CORES = 2
CHIPS = 32
OWNED = HEAD // CHIPS

ROW_BY_ROW = (((1,), (1,)), ((), ()))
COL_BY_COL = (((0,), (0,)), ((), ()))


def dot(a, b):
    return jnp.dot(a, b, preferred_element_type=F32)


def dot_on(a, b, dims):
    return lax.dot_general(a, b, dims, preferred_element_type=F32)


def any_spec():
    return pl.BlockSpec(memory_space=pl.ANY)


def sigmoid(x):
    return 0.5 * jnp.tanh(0.5 * x) + 0.5


def vmem_spec():
    return pl.BlockSpec(memory_space=pltpu.VMEM)


def grads_body(where, k_hbm, v_hbm, rate_ref, gate_hbm, lift_hbm, down_hbm, out_ref, k_ref, v_ref, fast, sems):
    head = where[0]
    tokens = k_ref.shape[0]
    half = tokens // 2
    column = pl.ds(pl.multiple_of(head * HEAD, HEAD), HEAD)
    moves = []

    def fetch(source, target):
        copy = pltpu.make_async_copy(source, target, sems.at[len(moves)])
        copy.start()
        moves.append(copy)
        return copy

    def rows_of(n):
        return pl.ds(n * half, half)

    waits = {
        "k0": fetch(k_hbm.at[rows_of(0), column], k_ref.at[rows_of(0)]),
        "gate": fetch(gate_hbm.at[head], fast.at[0]),
        "lift": fetch(lift_hbm.at[head], fast.at[1]),
        "v0": fetch(v_hbm.at[rows_of(0), column], v_ref.at[rows_of(0)]),
        "down": fetch(down_hbm.at[head], fast.at[2]),
        "k1": fetch(k_hbm.at[rows_of(1), column], k_ref.at[rows_of(1)]),
        "v1": fetch(v_hbm.at[rows_of(1), column], v_ref.at[rows_of(1)]),
    }
    rates = jnp.where(head == 0, rate_ref[0:1, :], rate_ref[1:2, :])
    rate_col = jnp.broadcast_to(rates, (128, tokens)).T[:, :1]
    waits["k0"].wait()
    waits["gate"].wait()
    gate = fast[0].astype(BF)
    into_gate = into_lift = down_sum = None
    lift = down = None
    for n in range(2):
        rows = slice(n * half, (n + 1) * half)
        if n:
            waits["k1"].wait()
        keys = k_ref[rows, :]
        gate_pre = dot(keys, gate)
        sig = sigmoid(gate_pre)
        activated = gate_pre * sig
        slope = sig + activated * (1.0 - sig)
        if lift is None:
            waits["lift"].wait()
            lift = fast[1].astype(BF)
        lift_pre = dot(keys, lift)
        hidden = (activated * lift_pre).astype(BF)
        slope = lift_pre * slope
        waits["v1" if n else "v0"].wait()
        target = (-rate_col[rows, :] * v_ref[rows, :].astype(F32)).astype(BF)
        if down is None:
            waits["down"].wait()
            down = fast[2].astype(BF)
        back_hidden = dot_on(target, down, ROW_BY_ROW)
        back_gate = (back_hidden * slope).astype(BF)
        back_lift = (back_hidden * activated).astype(BF)
        parts = (
            dot_on(keys, back_gate, COL_BY_COL),
            dot_on(keys, back_lift, COL_BY_COL),
            dot_on(hidden, target, COL_BY_COL),
        )
        if n == 0:
            into_gate, into_lift, down_sum = parts
        else:
            for m, (first, second) in enumerate(zip((into_gate, into_lift, down_sum), parts)):
                total = (first + second).astype(out_ref.dtype)
                out_ref[:, m * OWNED : (m + 1) * OWNED, :] = total.reshape(CHIPS, OWNED, HEAD)


def head_grads(which, keys, values, rates, gate, lift, down, dtype):
    tokens = keys.shape[0]
    return pl.pallas_call(
        grads_body,
        out_shape=jax.ShapeDtypeStruct((CHIPS, 3 * OWNED, HEAD), dtype),
        grid_spec=pltpu.PrefetchScalarGridSpec(
            num_scalar_prefetch=1,
            grid=(1,),
            in_specs=[
                any_spec(),
                any_spec(),
                pl.BlockSpec((2, tokens), lambda i, w: (0, 0)),
                any_spec(),
                any_spec(),
                any_spec(),
            ],
            out_specs=vmem_spec(),
            scratch_shapes=[
                pltpu.VMEM((tokens, HEAD), BF),
                pltpu.VMEM((tokens, HEAD), BF),
                pltpu.VMEM((3, HEAD, HEAD), F32),
                pltpu.SemaphoreType.DMA((7,)),
            ],
        ),
        compiler_params=pltpu.CompilerParams(vmem_limit_bytes=30 * MIB),
        name="head_grads",
    )(which, keys, values, rates, gate, lift, down)


def renewed_weights(which, grads, fast):
    count = len(fast)

    def body(where, g_ref, *refs):
        fast_hbm, (out_ref, olds, sems) = refs[:count], refs[count:]
        copies = [
            pltpu.make_async_copy(ref.at[where[0]], olds.at[i], sems.at[i])
            for i, ref in enumerate(fast_hbm)
        ]
        for copy in copies:
            copy.start()
        diagonal = jnp.where(
            lax.broadcasted_iota(jnp.int32, (HEAD, HEAD), 0)
            == lax.broadcasted_iota(jnp.int32, (HEAD, HEAD), 1),
            COEF_A,
            0.0,
        )
        iterates, grams = [], []
        for i in range(count):
            g = g_ref[:, i * OWNED : (i + 1) * OWNED, :].reshape(HEAD, HEAD)
            wide = g.astype(F32)
            gram = dot_on(g, g, COL_BY_COL)
            squares = jnp.sum(wide * wide, axis=0, keepdims=True)
            inverse = lax.rsqrt(jnp.sum(squares, axis=1, keepdims=True) + EPSILON)
            iterates.append((wide * inverse).astype(BF))
            grams.append(gram * (inverse * inverse))
        for sweep in range(NS_STEPS):
            polys = []
            for i in range(count):
                half = grams[i].astype(BF)
                square = dot(half, half)
                polys.append((diagonal + COEF_B * grams[i] + COEF_C * square).astype(BF))
            for i in range(count):
                iterates[i] = dot(iterates[i], polys[i]).astype(BF)
            if sweep + 1 < NS_STEPS:
                for i in range(count):
                    grams[i] = dot_on(iterates[i], iterates[i], COL_BY_COL)
        for i in range(count):
            copies[i].wait()
            old = olds[i]
            change = old - iterates[i].astype(F32)
            old_square = jnp.sum(old * old, axis=0, keepdims=True)
            new_square = jnp.sum(change * change, axis=0, keepdims=True)
            out_ref[i * HEAD : (i + 1) * HEAD, :] = (
                change * jnp.sqrt(old_square / (new_square + EPSILON))
            ).astype(BF)

    return pl.pallas_call(
        body,
        out_shape=jax.ShapeDtypeStruct((count * HEAD, HEAD), BF),
        grid_spec=pltpu.PrefetchScalarGridSpec(
            num_scalar_prefetch=1,
            grid=(1,),
            in_specs=[vmem_spec()] + [any_spec()] * count,
            out_specs=vmem_spec(),
            scratch_shapes=[
                pltpu.VMEM((count, HEAD, HEAD), F32),
                pltpu.SemaphoreType.DMA((count,)),
            ],
        ),
        compiler_params=pltpu.CompilerParams(vmem_limit_bytes=24 * MIB),
    )(which, grads, *fast)


def cut_blocks(where, out_weight, values):
    columns = out_weight.shape[1] // 2
    rows = values.shape[0] // 2

    def body(w, weight_ref, value_ref, weight_out, late_out, early_out, sems):
        other = pl.ds(pl.multiple_of((1 - w[1]) * columns, columns), columns)
        copies = (
            pltpu.make_async_copy(value_ref.at[pl.ds(rows, rows)], late_out, sems.at[0]),
            pltpu.make_async_copy(weight_ref.at[:, other], weight_out, sems.at[1]),
            pltpu.make_async_copy(value_ref.at[pl.ds(0, rows)], early_out, sems.at[2]),
        )
        for copy in copies:
            copy.start()
        for copy in copies:
            copy.wait()

    width = values.shape[1]
    return pl.pallas_call(
        body,
        out_shape=(
            pltpu.HBM((out_weight.shape[0], columns), BF),
            pltpu.HBM((rows, width), BF),
            pltpu.HBM((rows, width), BF),
        ),
        grid_spec=pltpu.PrefetchScalarGridSpec(
            num_scalar_prefetch=1,
            grid=(1,),
            in_specs=[any_spec(), any_spec()],
            out_specs=[any_spec(), any_spec(), any_spec()],
            scratch_shapes=[pltpu.SemaphoreType.DMA((3,))],
        ),
        name="cut_blocks",
    )(where, out_weight, values)


SPAN = WINDOW + CHUNK


def scores_body(flag, q_ref, edge_ref, key_ref, out_ref, span, sems):
    head, at = pl.program_id(0), pl.program_id(1)
    heads = pl.num_programs(0)
    tokens = key_ref.shape[0]

    def copies(h):
        column = pl.ds(pl.multiple_of(h * HEAD, HEAD), HEAD)
        return (
            pltpu.make_async_copy(
                edge_ref.at[:, column], span.at[h, pl.ds(0, WINDOW)], sems.at[h, 0]
            ),
            pltpu.make_async_copy(
                key_ref.at[:, column], span.at[h, pl.ds(WINDOW, tokens)], sems.at[h, 1]
            ),
        )

    @pl.when((head == 0) & (at == 0))
    def _():
        for copy in copies(0):
            copy.start()

    @pl.when(at == 0)
    def _():
        for copy in copies(head):
            copy.wait()

    @pl.when((at == 0) & (head + 1 < heads))
    def _():
        for copy in copies(head + 1):
            copy.start()

    keys = span[head, pl.ds(pl.multiple_of(at * CHUNK, CHUNK), SPAN), :]
    scores = dot_on(q_ref[...], keys, ROW_BY_ROW)
    row = lax.broadcasted_iota(jnp.int32, scores.shape, 0)
    col = lax.broadcasted_iota(jnp.int32, scores.shape, 1)
    first = jnp.where(flag[0] > 0, 0, WINDOW - at * CHUNK)
    allowed = (col > row) & (col <= row + WINDOW) & (col >= first)
    scores = jnp.where(allowed, scores, -jnp.inf)
    largest = jnp.max(scores, axis=1, keepdims=True)
    exponent = jnp.exp((scores - largest) * (HEAD ** (-0.5)))
    summed = jnp.sum(exponent, axis=1, keepdims=True)
    out_ref[...] = (exponent * (1.0 / summed)).astype(BF)


def probabilities(has_edge, queries, edge_keys, keys):
    tokens, width = queries.shape
    heads = width // HEAD
    return pl.pallas_call(
        scores_body,
        out_shape=jax.ShapeDtypeStruct((tokens, heads * SPAN), BF),
        grid_spec=pltpu.PrefetchScalarGridSpec(
            num_scalar_prefetch=1,
            grid=(heads, tokens // CHUNK),
            in_specs=[
                pl.BlockSpec((CHUNK, HEAD), lambda h, i, flag: (i, h)),
                any_spec(),
                any_spec(),
            ],
            out_specs=pl.BlockSpec((CHUNK, SPAN), lambda h, i, flag: (i, h)),
            scratch_shapes=[
                pltpu.VMEM((heads, WINDOW + tokens, HEAD), BF),
                pltpu.SemaphoreType.DMA((heads, 2)),
            ],
        ),
        compiler_params=pltpu.CompilerParams(
            dimension_semantics=("arbitrary", "arbitrary"), vmem_limit_bytes=24 * MIB
        ),
        name="probabilities",
    )(has_edge, queries, edge_keys, keys)


PIECE = 2 * CHUNK


def combined_piece(at, mirror, where, queries, probability, weights, gain, edges, values, after):
    from_edge = sum(edge.shape[0] for edge in edges)
    from_own = (at + 1) * PIECE

    def head_of(w):
        return 1 - w[0] if mirror else w[0]

    def body(w, q_hbm, p_hbm, w_ref, gain_ref, value_hbm, *refs):
        edge_hbm, (out_ref, q_ref, p_ref, span, sems) = refs[: len(edges)], refs[-5:]
        head = head_of(w)
        column = pl.ds(pl.multiple_of(head * HEAD, HEAD), HEAD)
        chances = pl.ds(pl.multiple_of(head * SPAN, SPAN), SPAN)
        rows = pl.ds(at * PIECE, PIECE)
        moves = [
            (q_hbm.at[rows, column], q_ref),
            (p_hbm.at[rows, chances], p_ref),
            (value_hbm.at[pl.ds(0, from_own), column], span.at[pl.ds(from_edge, from_own)]),
        ]
        start = 0
        for edge in edge_hbm:
            count = edge.shape[0]
            moves.append((edge.at[:, column], span.at[pl.ds(start, count)]))
            start += count
        copies = [
            pltpu.make_async_copy(source, target, sems.at[n])
            for n, (source, target) in enumerate(moves)
        ]
        for copy in copies:
            copy.start()
        copies[0].wait()
        q = q_ref[...]
        gate = dot(q, w_ref[0:HEAD, :])
        lift = dot(q, w_ref[HEAD : 2 * HEAD, :])
        hidden = (gate * sigmoid(gate) * lift).astype(BF)
        out = dot(hidden, w_ref[2 * HEAD :, :])
        mean_square = jnp.mean(out * out, axis=1, keepdims=True)
        scale = jnp.where(head == 0, gain_ref[0:1, :], gain_ref[1:2, :])
        normed = out * lax.rsqrt(mean_square + EPSILON) * scale
        for copy in copies[1:]:
            copy.wait()
        for part in range(PIECE // CHUNK):
            rows = slice(part * CHUNK, (part + 1) * CHUNK)
            attended = dot(p_ref[rows, :], span[part * CHUNK : part * CHUNK + SPAN, :])
            out_ref[rows, :] = (attended + normed[rows, :]).astype(BF)

    return pl.pallas_call(
        body,
        out_shape=jax.ShapeDtypeStruct((PIECE, HEAD), BF),
        grid_spec=pltpu.PrefetchScalarGridSpec(
            num_scalar_prefetch=1,
            grid=(1,),
            in_specs=[any_spec(), any_spec(), vmem_spec(), vmem_spec(), any_spec()]
            + [any_spec()] * (len(edges) + len(after)),
            out_specs=vmem_spec(),
            scratch_shapes=[
                pltpu.VMEM((PIECE, HEAD), BF),
                pltpu.VMEM((PIECE, SPAN), BF),
                pltpu.VMEM((WINDOW + PIECE, HEAD), BF),
                pltpu.SemaphoreType.DMA((3 + len(edges),)),
            ],
        ),
        compiler_params=pltpu.CompilerParams(vmem_limit_bytes=16 * MIB),
    )(where, queries, probability, weights, gain, values, *edges, *after)


def project_piece(where, combined, first_arrived, out_weight, other_weight):
    columns = out_weight.shape[1] // 2
    step = columns // 2

    def body(w, a_ref, b_ref, c_ref, wa_ref, wb_ref, wc_ref, out_ref):
        out_ref[...] = (
            dot(a_ref[...], wa_ref[...]) + dot(b_ref[...], wb_ref[...]) + dot(c_ref[...], wc_ref[...])
        )

    rows = pl.BlockSpec((PIECE, HEAD), lambda i, w: (0, 0))
    return pl.pallas_call(
        body,
        out_shape=jax.ShapeDtypeStruct((PIECE, columns), F32),
        grid_spec=pltpu.PrefetchScalarGridSpec(
            num_scalar_prefetch=1,
            grid=(2,),
            in_specs=[
                rows,
                rows,
                rows,
                pl.BlockSpec((HEAD, step), lambda i, w: (w[0], 2 * w[1] + i)),
                pl.BlockSpec((HEAD, step), lambda i, w: (1 - w[0], 2 * w[1] + i)),
                pl.BlockSpec((HEAD, step), lambda i, w: (w[0], i)),
            ],
            out_specs=pl.BlockSpec((PIECE, step), lambda i, w: (0, i)),
        ),
        compiler_params=pltpu.CompilerParams(vmem_limit_bytes=16 * MIB),
        name="project",
    )(where, *combined, first_arrived, out_weight, out_weight, other_weight)


def finish_piece(at, tokens, where, partial, last_arrived, other_weight, before):
    columns = partial.shape[1]
    step = columns // 2

    def body(w, acc_ref, a_ref, wa_ref, *refs):
        here = pl.ds(pl.multiple_of(pl.program_id(0) * step, step), step)
        rows = pl.ds(pl.multiple_of((1 - w[0]) * HEAD, HEAD), HEAD)
        refs[-1][...] = (acc_ref[:, here] + dot(a_ref[...], wa_ref[rows, here])).astype(BF)

    held = () if before is None else (before,)
    return pl.pallas_call(
        body,
        out_shape=jax.ShapeDtypeStruct((tokens, columns), BF),
        grid_spec=pltpu.PrefetchScalarGridSpec(
            num_scalar_prefetch=1,
            grid=(2,),
            in_specs=[vmem_spec(), vmem_spec(), vmem_spec()] + [any_spec()] * len(held),
            out_specs=pl.BlockSpec((PIECE, step), lambda i, w: (at, i)),
        ),
        compiler_params=pltpu.CompilerParams(vmem_limit_bytes=12 * MIB),
        input_output_aliases={4: 0} if held else {},
    )(where, partial, last_arrived, other_weight, *held)


def partner(value, flip):
    count = lax.axis_size("seq")
    return lax.ppermute(value, "seq", [(i, i ^ flip) for i in range(count)])


def over_chips(value):
    groups = [[p * CORES + r for p in range(CHIPS)] for r in range(CORES)]
    return lax.all_to_all(value, "seq", 0, 0, tiled=True, axis_index_groups=groups)


def to_all_chips(part):
    return over_chips(jnp.broadcast_to(part[None], (CHIPS, *part.shape)))


def shards(
    queries,
    key_rows,
    value_rows,
    token_rates,
    gate_fast,
    lift_fast,
    down_fast,
    memory_gain,
    out_weight,
):
    queries, key_rows, value_rows, token_rates, gate_fast, lift_fast, down_fast, out_weight = (
        pltpu.with_memory_space_constraint(x, pltpu.HBM)
        for x in (
            queries,
            key_rows,
            value_rows,
            token_rates,
            gate_fast,
            lift_fast,
            down_fast,
            out_weight,
        )
    )
    tokens_here = queries.shape[0]
    seq = lax.axis_index("seq")
    core = (seq % 2).astype(jnp.int32)
    head = lax.axis_index("head").astype(jnp.int32)
    where = jnp.stack([core, head])
    mirrored = jnp.stack([1 - core, head])
    has_edge = jnp.where(seq > 0, 1, 0).astype(jnp.int32).reshape(1)

    fast = (gate_fast, lift_fast, down_fast)
    tokens = (key_rows, value_rows, token_rates)
    grads_send = head_grads(mirrored, *tokens, *fast, BF)
    grads_got = partner(grads_send, 1)
    grads_mine = head_grads(where, *tokens, *fast, F32)

    count = lax.axis_size("seq")
    along = [(i, i + 1) for i in range(count - 1)]
    edge_keys = lax.ppermute(key_rows, "seq", along)
    other_columns, late, early = cut_blocks(where, out_weight, value_rows)
    edge_late = lax.ppermute(late, "seq", along)
    edge_early = lax.ppermute(early, "seq", along)
    pairs = [
        (group * count + i, (1 - group) * count + (i ^ 2)) for group in range(2) for i in range(count)
    ]
    other_weight = lax.ppermute(other_columns, ("head", "seq"), pairs)

    chip_sum = (grads_mine + grads_got.astype(F32)).astype(BF)
    slices = over_chips(chip_sum)
    part = slices.astype(F32).sum(axis=0).astype(BF)
    grads = to_all_chips(part)

    weights_mine = renewed_weights(where, grads, (gate_fast, lift_fast, down_fast))
    weights_theirs = partner(weights_mine, 1)

    probability = pltpu.with_memory_space_constraint(
        probabilities(has_edge, queries, edge_keys, key_rows), pltpu.HBM
    )

    pieces = tokens_here // PIECE
    head_pair = [(0, 1), (1, 0)]
    made, arrived, after = {}, {}, ()
    for at in reversed(range(pieces)):
        edges = (edge_late,) if at else (edge_early, edge_late)
        for mirror, weights in ((False, weights_mine), (True, weights_theirs)):
            piece = combined_piece(
                at, mirror, where, queries, probability, weights, memory_gain, edges, value_rows, after
            )
            made[mirror, at], after = piece, (piece,)
            arrived[mirror, at] = lax.ppermute(piece, "head", head_pair)
    out = None
    for at in reversed(range(pieces)):
        partial = project_piece(
            where,
            (made[False, at], made[True, at]),
            arrived[False, at],
            out_weight,
            other_weight,
        )
        out = finish_piece(at, tokens_here, where, partial, arrived[True, at], other_weight, out)
    return out


def solution(mesh):
    return jax.shard_map(
        shards,
        mesh=mesh,
        in_specs=(
            P("seq", "head"),
            P("seq", "head"),
            P("seq", "head"),
            P("head", "seq"),
            P("head", None, None),
            P("head", None, None),
            P("head", None, None),
            P("head", None),
            P("head", None),
        ),
        out_specs=P("seq", "head"),
        check_vma=False,
    )
```

```python
import jax
import jax.numpy as jnp
from jax import lax
from jax.experimental import pallas as pl
from jax.experimental.pallas import tpu as pltpu
from jax.sharding import PartitionSpec as P


HEAD = 512
WINDOW = 1024
NS_STEPS = 2
COEF_A = 3.4445
COEF_B = -4.775
COEF_C = 2.0315
EPSILON = 1e-06

CHUNK = 256
BF = jnp.bfloat16
F32 = jnp.float32
MIB = 1 << 20

PLANE = 4
PLANES = 16

ROW_BY_ROW = (((1,), (1,)), ((), ()))
COL_BY_COL = (((0,), (0,)), ((), ()))


def dot(a, b):
    return jnp.dot(a, b, preferred_element_type=F32)


def dot_on(a, b, dims):
    return lax.dot_general(a, b, dims, preferred_element_type=F32)


def any_spec():
    return pl.BlockSpec(memory_space=pl.ANY)


def sigmoid(x):
    return 0.5 * jnp.tanh(0.5 * x) + 0.5


def vmem_spec():
    return pl.BlockSpec(memory_space=pltpu.VMEM)


def grads_body(where, k_hbm, v_hbm, rate_ref, gate_hbm, lift_hbm, down_hbm, out_ref, k_ref, v_ref, fast, sems):
    head = where[0]
    tokens = k_ref.shape[0]
    half = tokens // 2
    column = pl.ds(pl.multiple_of(head * HEAD, HEAD), HEAD)
    moves = []

    def fetch(source, target):
        copy = pltpu.make_async_copy(source, target, sems.at[len(moves)])
        copy.start()
        moves.append(copy)
        return copy

    def rows_of(n):
        return pl.ds(n * half, half)

    waits = {
        "k0": fetch(k_hbm.at[rows_of(0), column], k_ref.at[rows_of(0)]),
        "gate": fetch(gate_hbm.at[head], fast.at[0]),
        "lift": fetch(lift_hbm.at[head], fast.at[1]),
        "v0": fetch(v_hbm.at[rows_of(0), column], v_ref.at[rows_of(0)]),
        "down": fetch(down_hbm.at[head], fast.at[2]),
        "k1": fetch(k_hbm.at[rows_of(1), column], k_ref.at[rows_of(1)]),
        "v1": fetch(v_hbm.at[rows_of(1), column], v_ref.at[rows_of(1)]),
    }
    rates = jnp.where(head == 0, rate_ref[0:1, :], rate_ref[1:2, :])
    rate_col = jnp.broadcast_to(rates, (128, tokens)).T[:, :1]
    waits["k0"].wait()
    waits["gate"].wait()
    gate = fast[0].astype(BF)
    into_gate = into_lift = down_sum = None
    lift = down = None
    for n in range(2):
        rows = slice(n * half, (n + 1) * half)
        if n:
            waits["k1"].wait()
        keys = k_ref[rows, :]
        gate_pre = dot(keys, gate)
        sig = sigmoid(gate_pre)
        activated = gate_pre * sig
        slope = sig + activated * (1.0 - sig)
        if lift is None:
            waits["lift"].wait()
            lift = fast[1].astype(BF)
        lift_pre = dot(keys, lift)
        hidden = (activated * lift_pre).astype(BF)
        slope = lift_pre * slope
        waits["v1" if n else "v0"].wait()
        target = (-rate_col[rows, :] * v_ref[rows, :].astype(F32)).astype(BF)
        if down is None:
            waits["down"].wait()
            down = fast[2].astype(BF)
        back_hidden = dot_on(target, down, ROW_BY_ROW)
        back_gate = (back_hidden * slope).astype(BF)
        back_lift = (back_hidden * activated).astype(BF)
        parts = (
            dot_on(keys, back_gate, COL_BY_COL),
            dot_on(keys, back_lift, COL_BY_COL),
            dot_on(hidden, target, COL_BY_COL),
        )
        if n == 0:
            into_gate, into_lift, down_sum = parts
        else:
            for m, (first, second) in enumerate(zip((into_gate, into_lift, down_sum), parts)):
                out_ref[m * HEAD : (m + 1) * HEAD, :] = (first + second).astype(out_ref.dtype)


def head_grads(which, keys, values, rates, gate, lift, down, dtype):
    tokens = keys.shape[0]
    return pl.pallas_call(
        grads_body,
        out_shape=jax.ShapeDtypeStruct((3 * HEAD, HEAD), dtype),
        grid_spec=pltpu.PrefetchScalarGridSpec(
            num_scalar_prefetch=1,
            grid=(1,),
            in_specs=[
                any_spec(),
                any_spec(),
                pl.BlockSpec((2, tokens), lambda i, w: (0, 0)),
                any_spec(),
                any_spec(),
                any_spec(),
            ],
            out_specs=vmem_spec(),
            scratch_shapes=[
                pltpu.VMEM((tokens, HEAD), BF),
                pltpu.VMEM((tokens, HEAD), BF),
                pltpu.VMEM((3, HEAD, HEAD), F32),
                pltpu.SemaphoreType.DMA((7,)),
            ],
        ),
        compiler_params=pltpu.CompilerParams(vmem_limit_bytes=30 * MIB),
        name="head_grads",
    )(which, keys, values, rates, gate, lift, down)


def renew_body(where, g_hbm, gate_ref, lift_ref, down_ref, out_ref, g_ref, olds, sems):
    loads = [
        pltpu.make_async_copy(
            g_hbm.at[pl.ds(i * HEAD, HEAD)], g_ref.at[pl.ds(i * HEAD, HEAD)], sems.at[3 + i]
        )
        for i in range(3)
    ]
    for load in loads:
        load.start()
    copies = [
        pltpu.make_async_copy(ref.at[where[0]], olds.at[i], sems.at[i])
        for i, ref in enumerate((gate_ref, lift_ref, down_ref))
    ]
    eye = (
        lax.broadcasted_iota(jnp.int32, (HEAD, HEAD), 0)
        == lax.broadcasted_iota(jnp.int32, (HEAD, HEAD), 1)
    ).astype(F32)
    iterates, grams = [], []
    for i in range(3):
        loads[i].wait()
        if i == 2:
            for copy in copies:
                copy.start()
        g = g_ref[i * HEAD : (i + 1) * HEAD, :]
        wide = g.astype(F32)
        gram = dot_on(g, g, COL_BY_COL)
        squares = jnp.sum(wide * wide, axis=0, keepdims=True)
        inverse = lax.rsqrt(jnp.sum(squares, axis=1, keepdims=True) + EPSILON)
        iterates.append((wide * inverse).astype(BF))
        grams.append(gram * (inverse * inverse))
    for sweep in range(NS_STEPS):
        polys = []
        for i in range(3):
            half = grams[i].astype(BF)
            square = dot(half, half)
            polys.append((COEF_A * eye + COEF_B * grams[i] + COEF_C * square).astype(BF))
        for i in range(3):
            iterates[i] = dot(iterates[i], polys[i]).astype(BF)
        if sweep + 1 < NS_STEPS:
            for i in range(3):
                grams[i] = dot_on(iterates[i], iterates[i], COL_BY_COL)
    for i in range(3):
        copies[i].wait()
        old = olds[i]
        change = old - iterates[i].astype(F32)
        old_square = jnp.sum(old * old, axis=0, keepdims=True)
        new_square = jnp.sum(change * change, axis=0, keepdims=True)
        out_ref[i * HEAD : (i + 1) * HEAD, :] = (
            change * jnp.sqrt(old_square / (new_square + EPSILON))
        ).astype(BF)


def renewed_weights(which, grads, gate, lift, down):
    return pl.pallas_call(
        renew_body,
        out_shape=jax.ShapeDtypeStruct((3 * HEAD, HEAD), BF),
        grid_spec=pltpu.PrefetchScalarGridSpec(
            num_scalar_prefetch=1,
            grid=(1,),
            in_specs=[any_spec(), any_spec(), any_spec(), any_spec()],
            out_specs=vmem_spec(),
            scratch_shapes=[
                pltpu.VMEM((3 * HEAD, HEAD), BF),
                pltpu.VMEM((3, HEAD, HEAD), F32),
                pltpu.SemaphoreType.DMA((6,)),
            ],
        ),
        compiler_params=pltpu.CompilerParams(vmem_limit_bytes=24 * MIB),
        name="renewed_weights",
    )(which, grads, gate, lift, down)


def cut_blocks(where, out_weight, values):
    columns = out_weight.shape[1] // 2
    rows = values.shape[0] // 2

    def body(w, weight_ref, value_ref, weight_out, late_out, early_out, weight, value, sems):
        other = pl.ds(pl.multiple_of((1 - w[1]) * columns, columns), columns)
        low, high = pl.ds(0, rows), pl.ds(rows, rows)
        moves = (
            (weight_ref.at[:, other], weight, weight_out),
            (value_ref.at[high], value.at[high], late_out),
            (value_ref.at[low], value.at[low], early_out),
        )
        into = [pltpu.make_async_copy(a, b, sems.at[0, n]) for n, (a, b, _) in enumerate(moves)]
        back = [pltpu.make_async_copy(b, c, sems.at[1, n]) for n, (_, b, c) in enumerate(moves)]
        for copy in into:
            copy.start()
        for first, second in zip(into, back):
            first.wait()
            second.start()
        for copy in back:
            copy.wait()

    width = values.shape[1]
    return pl.pallas_call(
        body,
        out_shape=(
            pltpu.HBM((out_weight.shape[0], columns), BF),
            pltpu.HBM((rows, width), BF),
            pltpu.HBM((rows, width), BF),
        ),
        grid_spec=pltpu.PrefetchScalarGridSpec(
            num_scalar_prefetch=1,
            grid=(1,),
            in_specs=[any_spec(), any_spec()],
            out_specs=[any_spec(), any_spec(), any_spec()],
            scratch_shapes=[
                pltpu.VMEM((out_weight.shape[0], columns), BF),
                pltpu.VMEM(values.shape, BF),
                pltpu.SemaphoreType.DMA((2, 3)),
            ],
        ),
        compiler_params=pltpu.CompilerParams(vmem_limit_bytes=8 * MIB),
        name="cut_blocks",
    )(where, out_weight, values)


def add_blocks(mine, got):
    parts = 4
    rows = mine.shape[0] // parts

    def body(mine_ref, got_ref, out_hbm, held, sems):
        copies = []
        for n in range(parts):
            here = slice(n * rows, (n + 1) * rows)
            held[here, :] = (mine_ref[here, :] + got_ref[here, :].astype(F32)).astype(BF)
            where = pl.ds(n * rows, rows)
            copies.append(pltpu.make_async_copy(held.at[where], out_hbm.at[where], sems.at[n]))
            copies[-1].start()
        for copy in copies:
            copy.wait()

    return pl.pallas_call(
        body,
        out_shape=pltpu.HBM(mine.shape, BF),
        in_specs=[vmem_spec(), vmem_spec()],
        out_specs=any_spec(),
        scratch_shapes=[pltpu.VMEM(mine.shape, BF), pltpu.SemaphoreType.DMA((parts,))],
        compiler_params=pltpu.CompilerParams(vmem_limit_bytes=8 * MIB),
        name="add_blocks",
    )(mine, got)


def add_and_repeat(part, other):
    def body(part_ref, other_ref, out_hbm, held, sems):
        held[...] = (part_ref[...].astype(F32) + other_ref[...].astype(F32)).astype(BF)
        copies = [
            pltpu.make_async_copy(held, out_hbm.at[n], sems.at[n]) for n in range(PLANES)
        ]
        for copy in copies:
            copy.start()
        for copy in copies:
            copy.wait()

    return pl.pallas_call(
        body,
        out_shape=pltpu.HBM((PLANES, *part.shape), BF),
        in_specs=[vmem_spec(), vmem_spec()],
        out_specs=any_spec(),
        scratch_shapes=[pltpu.VMEM(part.shape, BF), pltpu.SemaphoreType.DMA((PLANES,))],
        compiler_params=pltpu.CompilerParams(vmem_limit_bytes=4 * MIB),
        name="add_and_repeat",
    )(part, other)


SPAN = WINDOW + CHUNK


def scores_body(flag, q_ref, edge_ref, key_ref, out_ref, span, sems):
    head, at = pl.program_id(0), pl.program_id(1)
    heads = pl.num_programs(0)
    tokens = key_ref.shape[0]

    def copies(h):
        column = pl.ds(pl.multiple_of(h * HEAD, HEAD), HEAD)
        return (
            pltpu.make_async_copy(
                edge_ref.at[:, column], span.at[h, pl.ds(0, WINDOW)], sems.at[h, 0]
            ),
            pltpu.make_async_copy(
                key_ref.at[:, column], span.at[h, pl.ds(WINDOW, tokens)], sems.at[h, 1]
            ),
        )

    @pl.when((head == 0) & (at == 0))
    def _():
        for copy in copies(0):
            copy.start()

    @pl.when(at == 0)
    def _():
        for copy in copies(head):
            copy.wait()

    @pl.when((at == 0) & (head + 1 < heads))
    def _():
        for copy in copies(head + 1):
            copy.start()

    keys = span[head, pl.ds(pl.multiple_of(at * CHUNK, CHUNK), SPAN), :]
    scores = dot_on(q_ref[...], keys, ROW_BY_ROW)
    row = lax.broadcasted_iota(jnp.int32, scores.shape, 0)
    col = lax.broadcasted_iota(jnp.int32, scores.shape, 1)
    first = jnp.where(flag[0] > 0, 0, WINDOW - at * CHUNK)
    allowed = (col > row) & (col <= row + WINDOW) & (col >= first)
    scores = jnp.where(allowed, scores, -jnp.inf)
    largest = jnp.max(scores, axis=1, keepdims=True)
    exponent = jnp.exp((scores - largest) * (HEAD ** (-0.5)))
    summed = jnp.sum(exponent, axis=1, keepdims=True)
    out_ref[...] = (exponent * (1.0 / summed)).astype(BF)


def probabilities(has_edge, queries, edge_keys, keys):
    tokens, width = queries.shape
    heads = width // HEAD
    return pl.pallas_call(
        scores_body,
        out_shape=jax.ShapeDtypeStruct((tokens, heads * SPAN), BF),
        grid_spec=pltpu.PrefetchScalarGridSpec(
            num_scalar_prefetch=1,
            grid=(heads, tokens // CHUNK),
            in_specs=[
                pl.BlockSpec((CHUNK, HEAD), lambda h, i, flag: (i, h)),
                any_spec(),
                any_spec(),
            ],
            out_specs=pl.BlockSpec((CHUNK, SPAN), lambda h, i, flag: (i, h)),
            scratch_shapes=[
                pltpu.VMEM((heads, WINDOW + tokens, HEAD), BF),
                pltpu.SemaphoreType.DMA((heads, 2)),
            ],
        ),
        compiler_params=pltpu.CompilerParams(
            dimension_semantics=("arbitrary", "arbitrary"), vmem_limit_bytes=24 * MIB
        ),
        name="probabilities",
    )(has_edge, queries, edge_keys, keys)


def combined_piece(start, rows, mirror, where, queries, probability, weights, gain, edges, values, after):
    half = WINDOW // 2
    from_edge = WINDOW - start
    from_own = start + rows
    edge_rows = ((start, half), (0, half)) if start < half else ((start - half, half),)
    edges = edges[-len(edge_rows) :]

    def head_of(w):
        return 1 - w[0] if mirror else w[0]

    def body(w, q_hbm, p_hbm, w_ref, gain_ref, value_hbm, *refs):
        edge_hbm, (out_ref, q_ref, p_ref, span, sems) = refs[: len(edges)], refs[-5:]
        head = head_of(w)
        column = pl.ds(pl.multiple_of(head * HEAD, HEAD), HEAD)
        chances = pl.ds(pl.multiple_of(head * SPAN, SPAN), SPAN)
        here = pl.ds(start, rows)
        moves = [
            (q_hbm.at[here, column], q_ref),
            (p_hbm.at[here, chances], p_ref),
            (value_hbm.at[pl.ds(0, from_own), column], span.at[pl.ds(from_edge, from_own)]),
        ]
        filled = 0
        for edge, (first, last) in zip(edge_hbm, edge_rows):
            count = last - first
            moves.append((edge.at[pl.ds(first, count), column], span.at[pl.ds(filled, count)]))
            filled += count
        copies = [
            pltpu.make_async_copy(source, target, sems.at[n])
            for n, (source, target) in enumerate(moves)
        ]
        for copy in copies:
            copy.start()
        copies[0].wait()
        q = q_ref[...]
        gate = dot(q, w_ref[0:HEAD, :])
        lift = dot(q, w_ref[HEAD : 2 * HEAD, :])
        hidden = (gate * sigmoid(gate) * lift).astype(BF)
        out = dot(hidden, w_ref[2 * HEAD :, :])
        mean_square = jnp.mean(out * out, axis=1, keepdims=True)
        scale = jnp.where(head == 0, gain_ref[0:1, :], gain_ref[1:2, :])
        normed = out * lax.rsqrt(mean_square + EPSILON) * scale
        for copy in copies[1:]:
            copy.wait()
        for part in range(rows // CHUNK):
            some = slice(part * CHUNK, (part + 1) * CHUNK)
            attended = dot(p_ref[some, :], span[part * CHUNK : part * CHUNK + SPAN, :])
            out_ref[some, :] = (attended + normed[some, :]).astype(BF)

    return pl.pallas_call(
        body,
        out_shape=jax.ShapeDtypeStruct((rows, HEAD), BF),
        grid_spec=pltpu.PrefetchScalarGridSpec(
            num_scalar_prefetch=1,
            grid=(1,),
            in_specs=[any_spec(), any_spec(), vmem_spec(), vmem_spec(), any_spec()]
            + [any_spec()] * (len(edges) + len(after)),
            out_specs=vmem_spec(),
            scratch_shapes=[
                pltpu.VMEM((rows, HEAD), BF),
                pltpu.VMEM((rows, SPAN), BF),
                pltpu.VMEM((WINDOW + rows, HEAD), BF),
                pltpu.SemaphoreType.DMA((3 + len(edges),)),
            ],
        ),
        compiler_params=pltpu.CompilerParams(vmem_limit_bytes=16 * MIB),
    )(where, queries, probability, weights, gain, values, *edges, *after)


def project_chunk(where, operands, out_weight, other_weight, after):
    columns = out_weight.shape[1] // 2
    step = columns // 2

    def body(w, a_ref, b_ref, c_ref, wa_ref, wb_ref, wc_ref, *refs):
        refs[-1][...] = (
            dot(a_ref[...], wa_ref[...]) + dot(b_ref[...], wb_ref[...]) + dot(c_ref[...], wc_ref[...])
        )

    def rows(block):
        return pl.BlockSpec((CHUNK, HEAD), lambda i, w: (block, 0))

    return pl.pallas_call(
        body,
        out_shape=jax.ShapeDtypeStruct((CHUNK, columns), F32),
        grid_spec=pltpu.PrefetchScalarGridSpec(
            num_scalar_prefetch=1,
            grid=(2,),
            in_specs=[rows(block) for _, block in operands]
            + [
                pl.BlockSpec((HEAD, step), lambda i, w: (w[0], 2 * w[1] + i)),
                pl.BlockSpec((HEAD, step), lambda i, w: (1 - w[0], 2 * w[1] + i)),
                pl.BlockSpec((HEAD, step), lambda i, w: (w[0], i)),
            ]
            + [any_spec()] * len(after),
            out_specs=pl.BlockSpec((CHUNK, step), lambda i, w: (0, i)),
        ),
        compiler_params=pltpu.CompilerParams(vmem_limit_bytes=16 * MIB),
        name="project",
    )(where, *(array for array, _ in operands), out_weight, out_weight, other_weight, *after)


def finish_chunk(at, tokens, where, partial, arrived, block, other_weight, before):
    columns = partial.shape[1]
    parts = 2
    step = columns // parts
    held = () if before is None else (before,)

    def body(w, acc_ref, a_ref, wa_ref, *refs):
        out_hbm, done, sems = refs[-3:]
        rows = pl.ds(pl.multiple_of((1 - w[0]) * HEAD, HEAD), HEAD)
        came = a_ref[block * CHUNK : (block + 1) * CHUNK, :]
        copies = []
        for n in range(parts):
            here = slice(n * step, (n + 1) * step)
            done[:, here] = (acc_ref[:, here] + dot(came, wa_ref[rows, here])).astype(BF)
            some = pl.ds(n * step, step)
            copies.append(
                pltpu.make_async_copy(
                    done.at[:, some], out_hbm.at[pl.ds(at * CHUNK, CHUNK), some], sems.at[n]
                )
            )
            copies[-1].start()
        for copy in copies:
            copy.wait()

    return pl.pallas_call(
        body,
        out_shape=jax.ShapeDtypeStruct((tokens, columns), BF),
        grid_spec=pltpu.PrefetchScalarGridSpec(
            num_scalar_prefetch=1,
            grid=(1,),
            in_specs=[vmem_spec(), vmem_spec(), vmem_spec()] + [any_spec()] * len(held),
            out_specs=any_spec(),
            scratch_shapes=[pltpu.VMEM((CHUNK, columns), BF), pltpu.SemaphoreType.DMA((parts,))],
        ),
        compiler_params=pltpu.CompilerParams(vmem_limit_bytes=12 * MIB),
        input_output_aliases={4: 0} if held else {},
    )(where, partial, arrived, other_weight, *held)


def partner(value, flip):
    count = lax.axis_size("seq")
    return lax.ppermute(value, "seq", [(i, i ^ flip) for i in range(count)])


def over_planes(value):
    groups = [[p * PLANE + r for p in range(PLANES)] for r in range(PLANE)]
    return lax.all_to_all(value, "seq", 0, 0, tiled=True, axis_index_groups=groups)


def shards(
    queries,
    key_rows,
    value_rows,
    token_rates,
    gate_fast,
    lift_fast,
    down_fast,
    memory_gain,
    out_weight,
):
    queries, key_rows, value_rows, token_rates, gate_fast, lift_fast, down_fast, out_weight = (
        pltpu.with_memory_space_constraint(x, pltpu.HBM)
        for x in (
            queries,
            key_rows,
            value_rows,
            token_rates,
            gate_fast,
            lift_fast,
            down_fast,
            out_weight,
        )
    )
    tokens_here = queries.shape[0]
    seq = lax.axis_index("seq")
    core = (seq % 2).astype(jnp.int32)
    head = lax.axis_index("head").astype(jnp.int32)
    where = jnp.stack([core, head])
    mirrored = jnp.stack([1 - core, head])
    has_edge = jnp.where(seq > 0, 1, 0).astype(jnp.int32).reshape(1)

    fast = (gate_fast, lift_fast, down_fast)
    tokens = (key_rows, value_rows, token_rates)
    grads_send = head_grads(mirrored, *tokens, *fast, BF)
    grads_got = partner(grads_send, 1)
    grads_mine = head_grads(where, *tokens, *fast, F32)

    count = lax.axis_size("seq")
    along = [(i, i + 1) for i in range(count - 1)]
    edge_keys = lax.ppermute(key_rows, "seq", along)
    other_columns, late, early = cut_blocks(where, out_weight, value_rows)
    edge_late = lax.ppermute(late, "seq", along)
    edge_early = lax.ppermute(early, "seq", along)
    pairs = [
        (group * count + i, (1 - group) * count + (i ^ 2)) for group in range(2) for i in range(count)
    ]
    other_weight = lax.ppermute(other_columns, ("head", "seq"), pairs)

    chip_sum = add_blocks(grads_mine, grads_got)
    slices = over_planes(chip_sum.reshape(PLANES, -1, HEAD))
    part = slices.astype(F32).sum(axis=0).astype(BF)
    other = partner(part, 2)
    spread = add_and_repeat(part, other)
    grads = over_planes(spread).reshape(3 * HEAD, HEAD)

    weights_mine = renewed_weights(where, grads, *fast)
    weights_theirs = partner(weights_mine, 1)

    probability = pltpu.with_memory_space_constraint(
        probabilities(has_edge, queries, edge_keys, key_rows), pltpu.HBM
    )

    head_pair = [(0, 1), (1, 0)]
    half = tokens_here // 2
    plan = (
        (half, CHUNK, False),
        (half + CHUNK, CHUNK, False),
        (half, half, True),
        (0, half, False),
        (0, CHUNK, True),
        (CHUNK, CHUNK, True),
    )
    made, arrived, after = {}, {}, ()
    for start, rows, mirror in plan:
        piece = combined_piece(
            start,
            rows,
            mirror,
            where,
            queries,
            probability,
            weights_theirs if mirror else weights_mine,
            memory_gain,
            (edge_early, edge_late),
            value_rows,
            after,
        )
        after = (piece,)
        came = lax.ppermute(piece, "head", head_pair)
        for block in range(rows // CHUNK):
            made[mirror, start // CHUNK + block] = (piece, block)
            arrived[mirror, start // CHUNK + block] = (came, block)
    out, after = None, ()
    for pair in ((2, 3), (0, 1)):
        partials = {}
        for at in pair:
            operands = (made[False, at], made[True, at], arrived[False, at])
            partials[at] = project_chunk(where, operands, out_weight, other_weight, after)
        for at in pair:
            out = finish_chunk(
                at, tokens_here, where, partials[at], *arrived[True, at], other_weight, out
            )
        after = (out,)
    return out


def solution(mesh):
    return jax.shard_map(
        shards,
        mesh=mesh,
        in_specs=(
            P("seq", "head"),
            P("seq", "head"),
            P("seq", "head"),
            P("head", "seq"),
            P("head", None, None),
            P("head", None, None),
            P("head", None, None),
            P("head", None),
            P("head", None),
        ),
        out_specs=P("seq", "head"),
        check_vma=False,
    )
```

```python
import jax
import jax.numpy as jnp
from jax import lax
from jax.experimental import pallas as pl
from jax.experimental.pallas import tpu as pltpu
from jax.sharding import PartitionSpec as P


HEAD = 512
WINDOW = 1024
NS_STEPS = 2
COEF_A = 3.4445
COEF_B = -4.775
COEF_C = 2.0315
EPSILON = 1e-06

CHUNK = 256
BF = jnp.bfloat16
F32 = jnp.float32
MIB = 1 << 20

PLANE = 4
PLANES = 16

ROW_BY_ROW = (((1,), (1,)), ((), ()))
COL_BY_COL = (((0,), (0,)), ((), ()))


def dot(a, b):
    return jnp.dot(a, b, preferred_element_type=F32)


def dot_on(a, b, dims):
    return lax.dot_general(a, b, dims, preferred_element_type=F32)


def any_spec():
    return pl.BlockSpec(memory_space=pl.ANY)


def sigmoid(x):
    return 1.0 / (1.0 + jnp.exp(-x))


def vmem_spec():
    return pl.BlockSpec(memory_space=pltpu.VMEM)


def grads_body(where, k_hbm, v_hbm, rate_ref, gate_hbm, lift_hbm, down_hbm, out_ref, k_ref, v_ref, fast, sems):
    head = where[0]
    tokens = k_ref.shape[0]
    half = tokens // 2
    column = pl.ds(pl.multiple_of(head * HEAD, HEAD), HEAD)
    moves = []

    def fetch(source, target):
        copy = pltpu.make_async_copy(source, target, sems.at[len(moves)])
        copy.start()
        moves.append(copy)
        return copy

    def rows_of(n):
        return pl.ds(n * half, half)

    waits = {
        "k0": fetch(k_hbm.at[rows_of(0), column], k_ref.at[rows_of(0)]),
        "gate": fetch(gate_hbm.at[head], fast.at[0]),
        "lift": fetch(lift_hbm.at[head], fast.at[1]),
        "v0": fetch(v_hbm.at[rows_of(0), column], v_ref.at[rows_of(0)]),
        "down": fetch(down_hbm.at[head], fast.at[2]),
        "k1": fetch(k_hbm.at[rows_of(1), column], k_ref.at[rows_of(1)]),
        "v1": fetch(v_hbm.at[rows_of(1), column], v_ref.at[rows_of(1)]),
    }
    rates = jnp.where(head == 0, rate_ref[0:1, :], rate_ref[1:2, :])
    rate_col = jnp.broadcast_to(rates, (128, tokens)).T[:, :1]
    waits["k0"].wait()
    waits["gate"].wait()
    gate = fast[0].astype(BF)
    into_gate = into_lift = down_sum = None
    lift = down = None
    for n in range(2):
        rows = slice(n * half, (n + 1) * half)
        if n:
            waits["k1"].wait()
        keys = k_ref[rows, :]
        gate_pre = dot(keys, gate)
        sig = sigmoid(gate_pre)
        activated = gate_pre * sig
        slope = sig + activated * (1.0 - sig)
        if lift is None:
            waits["lift"].wait()
            lift = fast[1].astype(BF)
        lift_pre = dot(keys, lift)
        hidden = (activated * lift_pre).astype(BF)
        slope = lift_pre * slope
        waits["v1" if n else "v0"].wait()
        target = (-rate_col[rows, :] * v_ref[rows, :].astype(F32)).astype(BF)
        if down is None:
            waits["down"].wait()
            down = fast[2].astype(BF)
        back_hidden = dot_on(target, down, ROW_BY_ROW)
        back_gate = (back_hidden * slope).astype(BF)
        back_lift = (back_hidden * activated).astype(BF)
        parts = (
            dot_on(keys, back_gate, COL_BY_COL),
            dot_on(keys, back_lift, COL_BY_COL),
            dot_on(hidden, target, COL_BY_COL),
        )
        if n == 0:
            into_gate, into_lift, down_sum = parts
        else:
            for m, (first, second) in enumerate(zip((into_gate, into_lift, down_sum), parts)):
                out_ref[m * HEAD : (m + 1) * HEAD, :] = (first + second).astype(out_ref.dtype)


def head_grads(which, keys, values, rates, gate, lift, down, dtype):
    tokens = keys.shape[0]
    return pl.pallas_call(
        grads_body,
        out_shape=jax.ShapeDtypeStruct((3 * HEAD, HEAD), dtype),
        grid_spec=pltpu.PrefetchScalarGridSpec(
            num_scalar_prefetch=1,
            grid=(1,),
            in_specs=[
                any_spec(),
                any_spec(),
                pl.BlockSpec((2, tokens), lambda i, w: (0, 0)),
                any_spec(),
                any_spec(),
                any_spec(),
            ],
            out_specs=vmem_spec(),
            scratch_shapes=[
                pltpu.VMEM((tokens, HEAD), BF),
                pltpu.VMEM((tokens, HEAD), BF),
                pltpu.VMEM((3, HEAD, HEAD), F32),
                pltpu.SemaphoreType.DMA((7,)),
            ],
        ),
        compiler_params=pltpu.CompilerParams(vmem_limit_bytes=30 * MIB),
        name="head_grads",
    )(which, keys, values, rates, gate, lift, down)


def renew_body(where, g_hbm, gate_ref, lift_ref, down_ref, out_ref, g_ref, olds, sems):
    loads = [
        pltpu.make_async_copy(
            g_hbm.at[pl.ds(i * HEAD, HEAD)], g_ref.at[pl.ds(i * HEAD, HEAD)], sems.at[3 + i]
        )
        for i in range(3)
    ]
    for load in loads:
        load.start()
    copies = [
        pltpu.make_async_copy(ref.at[where[0]], olds.at[i], sems.at[i])
        for i, ref in enumerate((gate_ref, lift_ref, down_ref))
    ]
    eye = (
        lax.broadcasted_iota(jnp.int32, (HEAD, HEAD), 0)
        == lax.broadcasted_iota(jnp.int32, (HEAD, HEAD), 1)
    ).astype(F32)
    iterates, grams = [], []
    for i in range(3):
        loads[i].wait()
        if i == 2:
            for copy in copies:
                copy.start()
        g = g_ref[i * HEAD : (i + 1) * HEAD, :]
        wide = g.astype(F32)
        gram = dot_on(g, g, COL_BY_COL)
        squares = jnp.sum(wide * wide, axis=0, keepdims=True)
        inverse = lax.rsqrt(jnp.sum(squares, axis=1, keepdims=True) + EPSILON)
        iterates.append((wide * inverse).astype(BF))
        grams.append(gram * (inverse * inverse))
    for sweep in range(NS_STEPS):
        polys = []
        for i in range(3):
            half = grams[i].astype(BF)
            square = dot(half, half)
            polys.append((COEF_A * eye + COEF_B * grams[i] + COEF_C * square).astype(BF))
        for i in range(3):
            iterates[i] = dot(iterates[i], polys[i]).astype(BF)
        if sweep + 1 < NS_STEPS:
            for i in range(3):
                grams[i] = dot_on(iterates[i], iterates[i], COL_BY_COL)
    for i in range(3):
        copies[i].wait()
        old = olds[i]
        change = old - iterates[i].astype(F32)
        old_square = jnp.sum(old * old, axis=0, keepdims=True)
        new_square = jnp.sum(change * change, axis=0, keepdims=True)
        out_ref[i * HEAD : (i + 1) * HEAD, :] = (
            change * jnp.sqrt(old_square / (new_square + EPSILON))
        ).astype(BF)


def renewed_weights(which, grads, gate, lift, down):
    return pl.pallas_call(
        renew_body,
        out_shape=jax.ShapeDtypeStruct((3 * HEAD, HEAD), BF),
        grid_spec=pltpu.PrefetchScalarGridSpec(
            num_scalar_prefetch=1,
            grid=(1,),
            in_specs=[any_spec(), any_spec(), any_spec(), any_spec()],
            out_specs=vmem_spec(),
            scratch_shapes=[
                pltpu.VMEM((3 * HEAD, HEAD), BF),
                pltpu.VMEM((3, HEAD, HEAD), F32),
                pltpu.SemaphoreType.DMA((6,)),
            ],
        ),
        compiler_params=pltpu.CompilerParams(vmem_limit_bytes=24 * MIB),
        name="renewed_weights",
    )(which, grads, gate, lift, down)


def cut_blocks(where, out_weight, values):
    columns = out_weight.shape[1] // 2
    rows = values.shape[0] // 2

    def body(w, weight_ref, value_ref, weight_out, late_out, early_out, weight, value, sems):
        other = pl.ds(pl.multiple_of((1 - w[1]) * columns, columns), columns)
        low, high = pl.ds(0, rows), pl.ds(rows, rows)
        moves = (
            (weight_ref.at[:, other], weight, weight_out),
            (value_ref.at[high], value.at[high], late_out),
            (value_ref.at[low], value.at[low], early_out),
        )
        into = [pltpu.make_async_copy(a, b, sems.at[0, n]) for n, (a, b, _) in enumerate(moves)]
        back = [pltpu.make_async_copy(b, c, sems.at[1, n]) for n, (_, b, c) in enumerate(moves)]
        for copy in into:
            copy.start()
        for first, second in zip(into, back):
            first.wait()
            second.start()
        for copy in back:
            copy.wait()

    width = values.shape[1]
    return pl.pallas_call(
        body,
        out_shape=(
            pltpu.HBM((out_weight.shape[0], columns), BF),
            pltpu.HBM((rows, width), BF),
            pltpu.HBM((rows, width), BF),
        ),
        grid_spec=pltpu.PrefetchScalarGridSpec(
            num_scalar_prefetch=1,
            grid=(1,),
            in_specs=[any_spec(), any_spec()],
            out_specs=[any_spec(), any_spec(), any_spec()],
            scratch_shapes=[
                pltpu.VMEM((out_weight.shape[0], columns), BF),
                pltpu.VMEM(values.shape, BF),
                pltpu.SemaphoreType.DMA((2, 3)),
            ],
        ),
        compiler_params=pltpu.CompilerParams(vmem_limit_bytes=8 * MIB),
        name="cut_blocks",
    )(where, out_weight, values)


def add_blocks(mine, got):
    parts = 4
    rows = mine.shape[0] // parts

    def body(mine_ref, got_ref, out_hbm, held, sems):
        copies = []
        for n in range(parts):
            here = slice(n * rows, (n + 1) * rows)
            held[here, :] = (mine_ref[here, :] + got_ref[here, :].astype(F32)).astype(BF)
            where = pl.ds(n * rows, rows)
            copies.append(pltpu.make_async_copy(held.at[where], out_hbm.at[where], sems.at[n]))
            copies[-1].start()
        for copy in copies:
            copy.wait()

    return pl.pallas_call(
        body,
        out_shape=pltpu.HBM(mine.shape, BF),
        in_specs=[vmem_spec(), vmem_spec()],
        out_specs=any_spec(),
        scratch_shapes=[pltpu.VMEM(mine.shape, BF), pltpu.SemaphoreType.DMA((parts,))],
        compiler_params=pltpu.CompilerParams(vmem_limit_bytes=8 * MIB),
        name="add_blocks",
    )(mine, got)


def sum_planes(slices):
    parts = 4
    step = PLANES // parts

    def body(slices_hbm, out_ref, held, sems):
        copies = []
        for n in range(parts):
            some = pl.ds(n * step, step)
            copies.append(pltpu.make_async_copy(slices_hbm.at[some], held.at[some], sems.at[n]))
            copies[-1].start()
        total = None
        for n in range(parts):
            copies[n].wait()
            for m in range(n * step, (n + 1) * step):
                plane = held[m].astype(F32)
                total = plane if total is None else total + plane
        out_ref[...] = total.astype(BF)

    return pl.pallas_call(
        body,
        out_shape=jax.ShapeDtypeStruct(slices.shape[1:], BF),
        in_specs=[any_spec()],
        out_specs=vmem_spec(),
        scratch_shapes=[pltpu.VMEM(slices.shape, BF), pltpu.SemaphoreType.DMA((parts,))],
        compiler_params=pltpu.CompilerParams(vmem_limit_bytes=8 * MIB),
        name="sum_planes",
    )(slices)


def add_and_repeat(part, other):
    def body(part_ref, other_ref, out_hbm, held, sems):
        held[...] = (part_ref[...].astype(F32) + other_ref[...].astype(F32)).astype(BF)
        copies = [
            pltpu.make_async_copy(held, out_hbm.at[n], sems.at[n]) for n in range(PLANES)
        ]
        for copy in copies:
            copy.start()
        for copy in copies:
            copy.wait()

    return pl.pallas_call(
        body,
        out_shape=pltpu.HBM((PLANES, *part.shape), BF),
        in_specs=[vmem_spec(), vmem_spec()],
        out_specs=any_spec(),
        scratch_shapes=[pltpu.VMEM(part.shape, BF), pltpu.SemaphoreType.DMA((PLANES,))],
        compiler_params=pltpu.CompilerParams(vmem_limit_bytes=4 * MIB),
        name="add_and_repeat",
    )(part, other)


SPAN = WINDOW + CHUNK


def scores_body(flag, q_ref, edge_ref, key_ref, out_ref, span, sems):
    head, at = pl.program_id(0), pl.program_id(1)
    heads = pl.num_programs(0)
    tokens = key_ref.shape[0]

    def copies(h):
        column = pl.ds(pl.multiple_of(h * HEAD, HEAD), HEAD)
        return (
            pltpu.make_async_copy(
                edge_ref.at[:, column], span.at[h, pl.ds(0, WINDOW)], sems.at[h, 0]
            ),
            pltpu.make_async_copy(
                key_ref.at[:, column], span.at[h, pl.ds(WINDOW, tokens)], sems.at[h, 1]
            ),
        )

    @pl.when((head == 0) & (at == 0))
    def _():
        for copy in copies(0):
            copy.start()

    @pl.when(at == 0)
    def _():
        for copy in copies(head):
            copy.wait()

    @pl.when((at == 0) & (head + 1 < heads))
    def _():
        for copy in copies(head + 1):
            copy.start()

    keys = span[head, pl.ds(pl.multiple_of(at * CHUNK, CHUNK), SPAN), :]
    scores = dot_on(q_ref[...], keys, ROW_BY_ROW)
    row = lax.broadcasted_iota(jnp.int32, scores.shape, 0)
    col = lax.broadcasted_iota(jnp.int32, scores.shape, 1)
    first = jnp.where(flag[0] > 0, 0, WINDOW - at * CHUNK)
    allowed = (col > row) & (col <= row + WINDOW) & (col >= first)
    scores = jnp.where(allowed, scores, -jnp.inf)
    largest = jnp.max(scores, axis=1, keepdims=True)
    exponent = jnp.exp((scores - largest) * (HEAD ** (-0.5)))
    summed = jnp.sum(exponent, axis=1, keepdims=True)
    out_ref[...] = (exponent * (1.0 / summed)).astype(BF)


def probabilities(has_edge, queries, edge_keys, keys):
    tokens, width = queries.shape
    heads = width // HEAD
    return pl.pallas_call(
        scores_body,
        out_shape=jax.ShapeDtypeStruct((tokens, heads * SPAN), BF),
        grid_spec=pltpu.PrefetchScalarGridSpec(
            num_scalar_prefetch=1,
            grid=(heads, tokens // CHUNK),
            in_specs=[
                pl.BlockSpec((CHUNK, HEAD), lambda h, i, flag: (i, h)),
                any_spec(),
                any_spec(),
            ],
            out_specs=pl.BlockSpec((CHUNK, SPAN), lambda h, i, flag: (i, h)),
            scratch_shapes=[
                pltpu.VMEM((heads, WINDOW + tokens, HEAD), BF),
                pltpu.SemaphoreType.DMA((heads, 2)),
            ],
        ),
        compiler_params=pltpu.CompilerParams(
            dimension_semantics=("arbitrary", "arbitrary"), vmem_limit_bytes=24 * MIB
        ),
        name="probabilities",
    )(has_edge, queries, edge_keys, keys)


def combined_piece(start, rows, mirror, where, queries, probability, weights, gain, edges, values, after):
    half = WINDOW // 2
    from_edge = WINDOW - start
    from_own = start + rows
    edge_rows = ((start, half), (0, half)) if start < half else ((start - half, half),)
    edges = edges[-len(edge_rows) :]

    def head_of(w):
        return 1 - w[0] if mirror else w[0]

    def body(w, q_hbm, p_hbm, w_ref, gain_ref, value_hbm, *refs):
        edge_hbm, (out_ref, q_ref, p_ref, span, sems) = refs[: len(edges)], refs[-5:]
        head = head_of(w)
        column = pl.ds(pl.multiple_of(head * HEAD, HEAD), HEAD)
        chances = pl.ds(pl.multiple_of(head * SPAN, SPAN), SPAN)
        here = pl.ds(start, rows)
        moves = [
            (q_hbm.at[here, column], q_ref),
            (p_hbm.at[here, chances], p_ref),
            (value_hbm.at[pl.ds(0, from_own), column], span.at[pl.ds(from_edge, from_own)]),
        ]
        filled = 0
        for edge, (first, last) in zip(edge_hbm, edge_rows):
            count = last - first
            moves.append((edge.at[pl.ds(first, count), column], span.at[pl.ds(filled, count)]))
            filled += count
        copies = [
            pltpu.make_async_copy(source, target, sems.at[n])
            for n, (source, target) in enumerate(moves)
        ]
        for copy in copies:
            copy.start()
        copies[0].wait()
        q = q_ref[...]
        gate = dot(q, w_ref[0:HEAD, :])
        lift = dot(q, w_ref[HEAD : 2 * HEAD, :])
        hidden = (gate * sigmoid(gate) * lift).astype(BF)
        out = dot(hidden, w_ref[2 * HEAD :, :])
        mean_square = jnp.mean(out * out, axis=1, keepdims=True)
        scale = jnp.where(head == 0, gain_ref[0:1, :], gain_ref[1:2, :])
        normed = out * lax.rsqrt(mean_square + EPSILON) * scale
        for copy in copies[1:]:
            copy.wait()
        for part in range(rows // CHUNK):
            some = slice(part * CHUNK, (part + 1) * CHUNK)
            attended = dot(p_ref[some, :], span[part * CHUNK : part * CHUNK + SPAN, :])
            out_ref[some, :] = (attended + normed[some, :]).astype(BF)

    return pl.pallas_call(
        body,
        out_shape=jax.ShapeDtypeStruct((rows, HEAD), BF),
        grid_spec=pltpu.PrefetchScalarGridSpec(
            num_scalar_prefetch=1,
            grid=(1,),
            in_specs=[any_spec(), any_spec(), vmem_spec(), vmem_spec(), any_spec()]
            + [any_spec()] * (len(edges) + len(after)),
            out_specs=vmem_spec(),
            scratch_shapes=[
                pltpu.VMEM((rows, HEAD), BF),
                pltpu.VMEM((rows, SPAN), BF),
                pltpu.VMEM((WINDOW + rows, HEAD), BF),
                pltpu.SemaphoreType.DMA((3 + len(edges),)),
            ],
        ),
        compiler_params=pltpu.CompilerParams(vmem_limit_bytes=16 * MIB),
    )(where, queries, probability, weights, gain, values, *edges, *after)


def project_chunk(where, operands, out_weight, other_weight, after):
    columns = out_weight.shape[1] // 2
    step = columns // 2

    def body(w, a_ref, b_ref, c_ref, wa_ref, wb_ref, wc_ref, *refs):
        refs[-1][...] = (
            dot(a_ref[...], wa_ref[...]) + dot(b_ref[...], wb_ref[...]) + dot(c_ref[...], wc_ref[...])
        )

    def rows(block):
        return pl.BlockSpec((CHUNK, HEAD), lambda i, w: (block, 0))

    return pl.pallas_call(
        body,
        out_shape=jax.ShapeDtypeStruct((CHUNK, columns), F32),
        grid_spec=pltpu.PrefetchScalarGridSpec(
            num_scalar_prefetch=1,
            grid=(2,),
            in_specs=[rows(block) for _, block in operands]
            + [
                pl.BlockSpec((HEAD, step), lambda i, w: (w[0], 2 * w[1] + i)),
                pl.BlockSpec((HEAD, step), lambda i, w: (1 - w[0], 2 * w[1] + i)),
                pl.BlockSpec((HEAD, step), lambda i, w: (w[0], i)),
            ]
            + [any_spec()] * len(after),
            out_specs=pl.BlockSpec((CHUNK, step), lambda i, w: (0, i)),
        ),
        compiler_params=pltpu.CompilerParams(vmem_limit_bytes=16 * MIB),
        name="project",
    )(where, *(array for array, _ in operands), out_weight, out_weight, other_weight, *after)


def finish_chunk(at, tokens, where, partial, arrived, block, other_weight, before):
    columns = partial.shape[1]
    parts = 2
    step = columns // parts
    held = () if before is None else (before,)

    def body(w, acc_ref, a_ref, wa_ref, *refs):
        out_hbm, done, sems = refs[-3:]
        rows = pl.ds(pl.multiple_of((1 - w[0]) * HEAD, HEAD), HEAD)
        came = a_ref[block * CHUNK : (block + 1) * CHUNK, :]
        copies = []
        for n in range(parts):
            here = slice(n * step, (n + 1) * step)
            done[:, here] = (acc_ref[:, here] + dot(came, wa_ref[rows, here])).astype(BF)
            some = pl.ds(n * step, step)
            copies.append(
                pltpu.make_async_copy(
                    done.at[:, some], out_hbm.at[pl.ds(at * CHUNK, CHUNK), some], sems.at[n]
                )
            )
            copies[-1].start()
        for copy in copies:
            copy.wait()

    return pl.pallas_call(
        body,
        out_shape=jax.ShapeDtypeStruct((tokens, columns), BF),
        grid_spec=pltpu.PrefetchScalarGridSpec(
            num_scalar_prefetch=1,
            grid=(1,),
            in_specs=[vmem_spec(), vmem_spec(), vmem_spec()] + [any_spec()] * len(held),
            out_specs=any_spec(),
            scratch_shapes=[pltpu.VMEM((CHUNK, columns), BF), pltpu.SemaphoreType.DMA((parts,))],
        ),
        compiler_params=pltpu.CompilerParams(vmem_limit_bytes=12 * MIB),
        input_output_aliases={4: 0} if held else {},
    )(where, partial, arrived, other_weight, *held)


def partner(value, flip):
    count = lax.axis_size("seq")
    return lax.ppermute(value, "seq", [(i, i ^ flip) for i in range(count)])


def over_planes(value):
    groups = [[p * PLANE + r for p in range(PLANES)] for r in range(PLANE)]
    return lax.all_to_all(value, "seq", 0, 0, tiled=True, axis_index_groups=groups)


def shards(
    queries,
    key_rows,
    value_rows,
    token_rates,
    gate_fast,
    lift_fast,
    down_fast,
    memory_gain,
    out_weight,
):
    queries, key_rows, value_rows, token_rates, gate_fast, lift_fast, down_fast, out_weight = (
        pltpu.with_memory_space_constraint(x, pltpu.HBM)
        for x in (
            queries,
            key_rows,
            value_rows,
            token_rates,
            gate_fast,
            lift_fast,
            down_fast,
            out_weight,
        )
    )
    tokens_here = queries.shape[0]
    seq = lax.axis_index("seq")
    core = (seq % 2).astype(jnp.int32)
    head = lax.axis_index("head").astype(jnp.int32)
    where = jnp.stack([core, head])
    mirrored = jnp.stack([1 - core, head])
    has_edge = jnp.where(seq > 0, 1, 0).astype(jnp.int32).reshape(1)

    fast = (gate_fast, lift_fast, down_fast)
    tokens = (key_rows, value_rows, token_rates)
    grads_send = head_grads(mirrored, *tokens, *fast, BF)
    grads_got = partner(grads_send, 1)
    grads_mine = head_grads(where, *tokens, *fast, F32)

    count = lax.axis_size("seq")
    along = [(i, i + 1) for i in range(count - 1)]
    edge_keys = lax.ppermute(key_rows, "seq", along)
    other_columns, late, early = cut_blocks(where, out_weight, value_rows)
    edge_late = lax.ppermute(late, "seq", along)
    edge_early = lax.ppermute(early, "seq", along)
    pairs = [
        (group * count + i, (1 - group) * count + (i ^ 2)) for group in range(2) for i in range(count)
    ]
    other_weight = lax.ppermute(other_columns, ("head", "seq"), pairs)

    chip_sum = add_blocks(grads_mine, grads_got)
    slices = over_planes(chip_sum.reshape(PLANES, -1, HEAD))
    part = sum_planes(slices)
    other = partner(part, 2)
    spread = add_and_repeat(part, other)
    grads = over_planes(spread).reshape(3 * HEAD, HEAD)

    weights_mine = renewed_weights(where, grads, *fast)
    weights_theirs = partner(weights_mine, 1)

    probability = pltpu.with_memory_space_constraint(
        probabilities(has_edge, queries, edge_keys, key_rows), pltpu.HBM
    )

    head_pair = [(0, 1), (1, 0)]
    half = tokens_here // 2
    plan = (
        (half, CHUNK, False),
        (half + CHUNK, CHUNK, False),
        (half, half, True),
        (0, half, False),
        (0, CHUNK, True),
        (CHUNK, CHUNK, True),
    )
    made, arrived, after = {}, {}, ()
    for start, rows, mirror in plan:
        piece = combined_piece(
            start,
            rows,
            mirror,
            where,
            queries,
            probability,
            weights_theirs if mirror else weights_mine,
            memory_gain,
            (edge_early, edge_late),
            value_rows,
            after,
        )
        after = (piece,)
        came = lax.ppermute(piece, "head", head_pair)
        for block in range(rows // CHUNK):
            made[mirror, start // CHUNK + block] = (piece, block)
            arrived[mirror, start // CHUNK + block] = (came, block)
    out, after = None, ()
    for pair in ((2, 3), (0, 1)):
        partials = {}
        for at in pair:
            operands = (made[False, at], made[True, at], arrived[False, at])
            partials[at] = project_chunk(where, operands, out_weight, other_weight, after)
        for at in pair:
            out = finish_chunk(
                at, tokens_here, where, partials[at], *arrived[True, at], other_weight, out
            )
        after = (out,)
    return out


def solution(mesh):
    return jax.shard_map(
        shards,
        mesh=mesh,
        in_specs=(
            P("seq", "head"),
            P("seq", "head"),
            P("seq", "head"),
            P("head", "seq"),
            P("head", None, None),
            P("head", None, None),
            P("head", None, None),
            P("head", None),
            P("head", None),
        ),
        out_specs=P("seq", "head"),
        check_vma=False,
    )
```

```python
import jax
import jax.numpy as jnp
from jax import lax
from jax.experimental import pallas as pl
from jax.experimental.pallas import tpu as pltpu
from jax.sharding import PartitionSpec as P


HEAD = 512
WINDOW = 1024
NS_STEPS = 2
COEF_A = 3.4445
COEF_B = -4.775
COEF_C = 2.0315
EPSILON = 1e-06

CHUNK = 256
BF = jnp.bfloat16
F32 = jnp.float32
MIB = 1 << 20

PLANE = 4
PLANES = 16

ROW_BY_ROW = (((1,), (1,)), ((), ()))
COL_BY_COL = (((0,), (0,)), ((), ()))


def dot(a, b):
    return jnp.dot(a, b, preferred_element_type=F32)


def dot_on(a, b, dims):
    return lax.dot_general(a, b, dims, preferred_element_type=F32)


def any_spec():
    return pl.BlockSpec(memory_space=pl.ANY)


def sigmoid(x):
    return 1.0 / (1.0 + jnp.exp(-x))


def vmem_spec():
    return pl.BlockSpec(memory_space=pltpu.VMEM)


def grads_body(where, k_hbm, v_hbm, rate_ref, gate_hbm, lift_hbm, down_hbm, out_ref, k_ref, v_ref, fast, sems):
    head = where[0]
    tokens = k_ref.shape[0]
    half = tokens // 2
    column = pl.ds(pl.multiple_of(head * HEAD, HEAD), HEAD)
    moves = []

    def fetch(source, target):
        copy = pltpu.make_async_copy(source, target, sems.at[len(moves)])
        copy.start()
        moves.append(copy)
        return copy

    def rows_of(n):
        return pl.ds(n * half, half)

    waits = {
        "k0": fetch(k_hbm.at[rows_of(0), column], k_ref.at[rows_of(0)]),
        "gate": fetch(gate_hbm.at[head], fast.at[0]),
        "lift": fetch(lift_hbm.at[head], fast.at[1]),
        "v0": fetch(v_hbm.at[rows_of(0), column], v_ref.at[rows_of(0)]),
        "down": fetch(down_hbm.at[head], fast.at[2]),
        "k1": fetch(k_hbm.at[rows_of(1), column], k_ref.at[rows_of(1)]),
        "v1": fetch(v_hbm.at[rows_of(1), column], v_ref.at[rows_of(1)]),
    }
    rates = jnp.where(head == 0, rate_ref[0:1, :], rate_ref[1:2, :])
    rate_col = jnp.broadcast_to(rates, (128, tokens)).T[:, :1]
    waits["k0"].wait()
    waits["gate"].wait()
    gate = fast[0].astype(BF)
    into_gate = into_lift = down_sum = None
    lift = down = None
    for n in range(2):
        rows = slice(n * half, (n + 1) * half)
        if n:
            waits["k1"].wait()
        keys = k_ref[rows, :]
        gate_pre = dot(keys, gate)
        sig = sigmoid(gate_pre)
        activated = gate_pre * sig
        slope = sig + activated * (1.0 - sig)
        if lift is None:
            waits["lift"].wait()
            lift = fast[1].astype(BF)
        lift_pre = dot(keys, lift)
        hidden = (activated * lift_pre).astype(BF)
        slope = lift_pre * slope
        waits["v1" if n else "v0"].wait()
        target = (-rate_col[rows, :] * v_ref[rows, :].astype(F32)).astype(BF)
        if down is None:
            waits["down"].wait()
            down = fast[2].astype(BF)
        back_hidden = dot_on(target, down, ROW_BY_ROW)
        back_gate = (back_hidden * slope).astype(BF)
        back_lift = (back_hidden * activated).astype(BF)
        parts = (
            dot_on(keys, back_gate, COL_BY_COL),
            dot_on(keys, back_lift, COL_BY_COL),
            dot_on(hidden, target, COL_BY_COL),
        )
        if n == 0:
            into_gate, into_lift, down_sum = parts
        else:
            for m, (first, second) in enumerate(zip((into_gate, into_lift, down_sum), parts)):
                out_ref[m * HEAD : (m + 1) * HEAD, :] = (first + second).astype(out_ref.dtype)


def head_grads(which, keys, values, rates, gate, lift, down, dtype):
    tokens = keys.shape[0]
    return pl.pallas_call(
        grads_body,
        out_shape=jax.ShapeDtypeStruct((3 * HEAD, HEAD), dtype),
        grid_spec=pltpu.PrefetchScalarGridSpec(
            num_scalar_prefetch=1,
            grid=(1,),
            in_specs=[
                any_spec(),
                any_spec(),
                pl.BlockSpec((2, tokens), lambda i, w: (0, 0)),
                any_spec(),
                any_spec(),
                any_spec(),
            ],
            out_specs=vmem_spec(),
            scratch_shapes=[
                pltpu.VMEM((tokens, HEAD), BF),
                pltpu.VMEM((tokens, HEAD), BF),
                pltpu.VMEM((3, HEAD, HEAD), F32),
                pltpu.SemaphoreType.DMA((7,)),
            ],
        ),
        compiler_params=pltpu.CompilerParams(vmem_limit_bytes=30 * MIB),
        name="head_grads",
    )(which, keys, values, rates, gate, lift, down)


def renew_body(where, g_hbm, gate_ref, lift_ref, down_ref, out_ref, g_ref, olds, sems):
    loads = [
        pltpu.make_async_copy(
            g_hbm.at[pl.ds(i * HEAD, HEAD)], g_ref.at[pl.ds(i * HEAD, HEAD)], sems.at[3 + i]
        )
        for i in range(3)
    ]
    for load in loads:
        load.start()
    copies = [
        pltpu.make_async_copy(ref.at[where[0]], olds.at[i], sems.at[i])
        for i, ref in enumerate((gate_ref, lift_ref, down_ref))
    ]
    eye = (
        lax.broadcasted_iota(jnp.int32, (HEAD, HEAD), 0)
        == lax.broadcasted_iota(jnp.int32, (HEAD, HEAD), 1)
    ).astype(F32)
    iterates, grams = [], []
    for i in range(3):
        loads[i].wait()
        if i == 2:
            for copy in copies:
                copy.start()
        g = g_ref[i * HEAD : (i + 1) * HEAD, :]
        wide = g.astype(F32)
        gram = dot_on(g, g, COL_BY_COL)
        squares = jnp.sum(wide * wide, axis=0, keepdims=True)
        inverse = lax.rsqrt(jnp.sum(squares, axis=1, keepdims=True) + EPSILON)
        iterates.append((wide * inverse).astype(BF))
        grams.append(gram * (inverse * inverse))
    for sweep in range(NS_STEPS):
        polys = []
        for i in range(3):
            half = grams[i].astype(BF)
            square = dot(half, half)
            polys.append((COEF_A * eye + COEF_B * grams[i] + COEF_C * square).astype(BF))
        for i in range(3):
            iterates[i] = dot(iterates[i], polys[i]).astype(BF)
        if sweep + 1 < NS_STEPS:
            for i in range(3):
                grams[i] = dot_on(iterates[i], iterates[i], COL_BY_COL)
    for i in range(3):
        copies[i].wait()
        old = olds[i]
        change = old - iterates[i].astype(F32)
        old_square = jnp.sum(old * old, axis=0, keepdims=True)
        new_square = jnp.sum(change * change, axis=0, keepdims=True)
        out_ref[i * HEAD : (i + 1) * HEAD, :] = (
            change * jnp.sqrt(old_square / (new_square + EPSILON))
        ).astype(BF)


def renewed_weights(which, grads, gate, lift, down):
    return pl.pallas_call(
        renew_body,
        out_shape=jax.ShapeDtypeStruct((3 * HEAD, HEAD), BF),
        grid_spec=pltpu.PrefetchScalarGridSpec(
            num_scalar_prefetch=1,
            grid=(1,),
            in_specs=[any_spec(), any_spec(), any_spec(), any_spec()],
            out_specs=vmem_spec(),
            scratch_shapes=[
                pltpu.VMEM((3 * HEAD, HEAD), BF),
                pltpu.VMEM((3, HEAD, HEAD), F32),
                pltpu.SemaphoreType.DMA((6,)),
            ],
        ),
        compiler_params=pltpu.CompilerParams(vmem_limit_bytes=24 * MIB),
        name="renewed_weights",
    )(which, grads, gate, lift, down)


def cut_blocks(where, out_weight, values):
    columns = out_weight.shape[1] // 2
    rows = values.shape[0] // 2

    def body(w, weight_ref, value_ref, weight_out, late_out, early_out, weight, value, sems):
        other = pl.ds(pl.multiple_of((1 - w[1]) * columns, columns), columns)
        mine = pl.ds(pl.multiple_of(w[0] * HEAD, HEAD), HEAD)
        low, high = pl.ds(0, rows), pl.ds(rows, rows)
        moves = (
            (weight_ref.at[mine, other], weight, weight_out),
            (value_ref.at[high], value.at[high], late_out),
            (value_ref.at[low], value.at[low], early_out),
        )
        into = [pltpu.make_async_copy(a, b, sems.at[0, n]) for n, (a, b, _) in enumerate(moves)]
        back = [pltpu.make_async_copy(b, c, sems.at[1, n]) for n, (_, b, c) in enumerate(moves)]
        for copy in into:
            copy.start()
        for first, second in zip(into, back):
            first.wait()
            second.start()
        for copy in back:
            copy.wait()

    width = values.shape[1]
    return pl.pallas_call(
        body,
        out_shape=(
            pltpu.HBM((HEAD, columns), BF),
            pltpu.HBM((rows, width), BF),
            pltpu.HBM((rows, width), BF),
        ),
        grid_spec=pltpu.PrefetchScalarGridSpec(
            num_scalar_prefetch=1,
            grid=(1,),
            in_specs=[any_spec(), any_spec()],
            out_specs=[any_spec(), any_spec(), any_spec()],
            scratch_shapes=[
                pltpu.VMEM((HEAD, columns), BF),
                pltpu.VMEM(values.shape, BF),
                pltpu.SemaphoreType.DMA((2, 3)),
            ],
        ),
        compiler_params=pltpu.CompilerParams(vmem_limit_bytes=8 * MIB),
        name="cut_blocks",
    )(where, out_weight, values)


def add_blocks(mine, got):
    parts = 4
    rows = mine.shape[0] // parts

    def body(mine_ref, got_ref, out_hbm, held, sems):
        copies = []
        for n in range(parts):
            here = slice(n * rows, (n + 1) * rows)
            held[here, :] = (mine_ref[here, :] + got_ref[here, :].astype(F32)).astype(BF)
            where = pl.ds(n * rows, rows)
            copies.append(pltpu.make_async_copy(held.at[where], out_hbm.at[where], sems.at[n]))
            copies[-1].start()
        for copy in copies:
            copy.wait()

    return pl.pallas_call(
        body,
        out_shape=pltpu.HBM(mine.shape, BF),
        in_specs=[vmem_spec(), vmem_spec()],
        out_specs=any_spec(),
        scratch_shapes=[pltpu.VMEM(mine.shape, BF), pltpu.SemaphoreType.DMA((parts,))],
        compiler_params=pltpu.CompilerParams(vmem_limit_bytes=8 * MIB),
        name="add_blocks",
    )(mine, got)


def sum_planes(slices):
    parts = 4
    step = PLANES // parts

    def body(slices_hbm, out_ref, held, sems):
        copies = []
        for n in range(parts):
            some = pl.ds(n * step, step)
            copies.append(pltpu.make_async_copy(slices_hbm.at[some], held.at[some], sems.at[n]))
            copies[-1].start()
        total = None
        for n in range(parts):
            copies[n].wait()
            for m in range(n * step, (n + 1) * step):
                plane = held[m].astype(F32)
                total = plane if total is None else total + plane
        out_ref[...] = total.astype(BF)

    return pl.pallas_call(
        body,
        out_shape=jax.ShapeDtypeStruct(slices.shape[1:], BF),
        in_specs=[any_spec()],
        out_specs=vmem_spec(),
        scratch_shapes=[pltpu.VMEM(slices.shape, BF), pltpu.SemaphoreType.DMA((parts,))],
        compiler_params=pltpu.CompilerParams(vmem_limit_bytes=8 * MIB),
        name="sum_planes",
    )(slices)


def add_and_repeat(part, other):
    def body(part_ref, other_ref, out_hbm, held, sems):
        held[...] = (part_ref[...].astype(F32) + other_ref[...].astype(F32)).astype(BF)
        copies = [
            pltpu.make_async_copy(held, out_hbm.at[n], sems.at[n]) for n in range(PLANES)
        ]
        for copy in copies:
            copy.start()
        for copy in copies:
            copy.wait()

    return pl.pallas_call(
        body,
        out_shape=pltpu.HBM((PLANES, *part.shape), BF),
        in_specs=[vmem_spec(), vmem_spec()],
        out_specs=any_spec(),
        scratch_shapes=[pltpu.VMEM(part.shape, BF), pltpu.SemaphoreType.DMA((PLANES,))],
        compiler_params=pltpu.CompilerParams(vmem_limit_bytes=4 * MIB),
        name="add_and_repeat",
    )(part, other)


SPAN = WINDOW + CHUNK


def scores_body(flag, q_ref, edge_ref, key_ref, out_ref, span, sems):
    head, at = pl.program_id(0), pl.program_id(1)
    heads = pl.num_programs(0)
    tokens = key_ref.shape[0]

    def copies(h):
        column = pl.ds(pl.multiple_of(h * HEAD, HEAD), HEAD)
        return (
            pltpu.make_async_copy(
                edge_ref.at[:, column], span.at[h, pl.ds(0, WINDOW)], sems.at[h, 0]
            ),
            pltpu.make_async_copy(
                key_ref.at[:, column], span.at[h, pl.ds(WINDOW, tokens)], sems.at[h, 1]
            ),
        )

    @pl.when((head == 0) & (at == 0))
    def _():
        for copy in copies(0):
            copy.start()

    @pl.when(at == 0)
    def _():
        for copy in copies(head):
            copy.wait()

    @pl.when((at == 0) & (head + 1 < heads))
    def _():
        for copy in copies(head + 1):
            copy.start()

    keys = span[head, pl.ds(pl.multiple_of(at * CHUNK, CHUNK), SPAN), :]
    scores = dot_on(q_ref[...], keys, ROW_BY_ROW)
    row = lax.broadcasted_iota(jnp.int32, scores.shape, 0)
    col = lax.broadcasted_iota(jnp.int32, scores.shape, 1)
    first = jnp.where(flag[0] > 0, 0, WINDOW - at * CHUNK)
    allowed = (col > row) & (col <= row + WINDOW) & (col >= first)
    scores = jnp.where(allowed, scores, -jnp.inf)
    largest = jnp.max(scores, axis=1, keepdims=True)
    exponent = jnp.exp((scores - largest) * (HEAD ** (-0.5)))
    summed = jnp.sum(exponent, axis=1, keepdims=True)
    out_ref[...] = (exponent * (1.0 / summed)).astype(BF)


def probabilities(has_edge, queries, edge_keys, keys):
    tokens, width = queries.shape
    heads = width // HEAD
    return pl.pallas_call(
        scores_body,
        out_shape=jax.ShapeDtypeStruct((tokens, heads * SPAN), BF),
        grid_spec=pltpu.PrefetchScalarGridSpec(
            num_scalar_prefetch=1,
            grid=(heads, tokens // CHUNK),
            in_specs=[
                pl.BlockSpec((CHUNK, HEAD), lambda h, i, flag: (i, h)),
                any_spec(),
                any_spec(),
            ],
            out_specs=pl.BlockSpec((CHUNK, SPAN), lambda h, i, flag: (i, h)),
            scratch_shapes=[
                pltpu.VMEM((heads, WINDOW + tokens, HEAD), BF),
                pltpu.SemaphoreType.DMA((heads, 2)),
            ],
        ),
        compiler_params=pltpu.CompilerParams(
            dimension_semantics=("arbitrary", "arbitrary"), vmem_limit_bytes=24 * MIB
        ),
        name="probabilities",
    )(has_edge, queries, edge_keys, keys)


def combined_piece(start, rows, mirror, where, queries, probability, weights, gain, edges, values, after):
    half = WINDOW // 2
    from_edge = WINDOW - start
    from_own = start + rows
    edge_rows = ((start, half), (0, half)) if start < half else ((start - half, half),)
    edges = edges[-len(edge_rows) :]

    def head_of(w):
        return 1 - w[0] if mirror else w[0]

    def body(w, q_hbm, p_hbm, w_ref, gain_ref, value_hbm, *refs):
        edge_hbm, (out_ref, q_ref, p_ref, span, sems) = refs[: len(edges)], refs[-5:]
        head = head_of(w)
        column = pl.ds(pl.multiple_of(head * HEAD, HEAD), HEAD)
        chances = pl.ds(pl.multiple_of(head * SPAN, SPAN), SPAN)
        here = pl.ds(start, rows)
        moves = [
            (q_hbm.at[here, column], q_ref),
            (p_hbm.at[here, chances], p_ref),
            (value_hbm.at[pl.ds(0, from_own), column], span.at[pl.ds(from_edge, from_own)]),
        ]
        filled = 0
        for edge, (first, last) in zip(edge_hbm, edge_rows):
            count = last - first
            moves.append((edge.at[pl.ds(first, count), column], span.at[pl.ds(filled, count)]))
            filled += count
        copies = [
            pltpu.make_async_copy(source, target, sems.at[n])
            for n, (source, target) in enumerate(moves)
        ]
        for copy in copies:
            copy.start()
        copies[0].wait()
        q = q_ref[...]
        gate = dot(q, w_ref[0:HEAD, :])
        lift = dot(q, w_ref[HEAD : 2 * HEAD, :])
        hidden = (gate * sigmoid(gate) * lift).astype(BF)
        out = dot(hidden, w_ref[2 * HEAD :, :])
        mean_square = jnp.mean(out * out, axis=1, keepdims=True)
        scale = jnp.where(head == 0, gain_ref[0:1, :], gain_ref[1:2, :])
        normed = out * lax.rsqrt(mean_square + EPSILON) * scale
        for copy in copies[1:]:
            copy.wait()
        for part in range(rows // CHUNK):
            some = slice(part * CHUNK, (part + 1) * CHUNK)
            attended = dot(p_ref[some, :], span[part * CHUNK : part * CHUNK + SPAN, :])
            out_ref[some, :] = (attended + normed[some, :]).astype(BF)

    return pl.pallas_call(
        body,
        out_shape=jax.ShapeDtypeStruct((rows, HEAD), BF),
        grid_spec=pltpu.PrefetchScalarGridSpec(
            num_scalar_prefetch=1,
            grid=(1,),
            in_specs=[any_spec(), any_spec(), vmem_spec(), vmem_spec(), any_spec()]
            + [any_spec()] * (len(edges) + len(after)),
            out_specs=vmem_spec(),
            scratch_shapes=[
                pltpu.VMEM((rows, HEAD), BF),
                pltpu.VMEM((rows, SPAN), BF),
                pltpu.VMEM((WINDOW + rows, HEAD), BF),
                pltpu.SemaphoreType.DMA((3 + len(edges),)),
            ],
        ),
        compiler_params=pltpu.CompilerParams(vmem_limit_bytes=16 * MIB),
    )(where, queries, probability, weights, gain, values, *edges, *after)


def project_chunk(where, operands, out_weight, other_weight, after):
    columns = out_weight.shape[1] // 2
    step = columns // 2

    def body(w, a_ref, b_ref, c_ref, wa_ref, wb_ref, wc_ref, *refs):
        refs[-1][...] = (
            dot(a_ref[...], wa_ref[...]) + dot(b_ref[...], wb_ref[...]) + dot(c_ref[...], wc_ref[...])
        )

    def rows(block):
        return pl.BlockSpec((CHUNK, HEAD), lambda i, w: (block, 0))

    return pl.pallas_call(
        body,
        out_shape=jax.ShapeDtypeStruct((CHUNK, columns), F32),
        grid_spec=pltpu.PrefetchScalarGridSpec(
            num_scalar_prefetch=1,
            grid=(2,),
            in_specs=[rows(block) for _, block in operands]
            + [
                pl.BlockSpec((HEAD, step), lambda i, w: (w[0], 2 * w[1] + i)),
                pl.BlockSpec((HEAD, step), lambda i, w: (1 - w[0], 2 * w[1] + i)),
                pl.BlockSpec((HEAD, step), lambda i, w: (0, i)),
            ]
            + [any_spec()] * len(after),
            out_specs=pl.BlockSpec((CHUNK, step), lambda i, w: (0, i)),
        ),
        compiler_params=pltpu.CompilerParams(vmem_limit_bytes=16 * MIB),
        name="project",
    )(where, *(array for array, _ in operands), out_weight, out_weight, other_weight, *after)


def finish_chunk(at, tokens, where, partial, arrived, block, other_weight, before):
    columns = partial.shape[1]
    parts = 2
    step = columns // parts
    held = () if before is None else (before,)

    def body(w, acc_ref, a_ref, wa_ref, *refs):
        out_hbm, done, sems = refs[-3:]
        came = a_ref[block * CHUNK : (block + 1) * CHUNK, :]
        copies = []
        for n in range(parts):
            here = slice(n * step, (n + 1) * step)
            done[:, here] = (acc_ref[:, here] + dot(came, wa_ref[:, here])).astype(BF)
            some = pl.ds(n * step, step)
            copies.append(
                pltpu.make_async_copy(
                    done.at[:, some], out_hbm.at[pl.ds(at * CHUNK, CHUNK), some], sems.at[n]
                )
            )
            copies[-1].start()
        for copy in copies:
            copy.wait()

    return pl.pallas_call(
        body,
        out_shape=jax.ShapeDtypeStruct((tokens, columns), BF),
        grid_spec=pltpu.PrefetchScalarGridSpec(
            num_scalar_prefetch=1,
            grid=(1,),
            in_specs=[vmem_spec(), vmem_spec(), vmem_spec()] + [any_spec()] * len(held),
            out_specs=any_spec(),
            scratch_shapes=[pltpu.VMEM((CHUNK, columns), BF), pltpu.SemaphoreType.DMA((parts,))],
        ),
        compiler_params=pltpu.CompilerParams(vmem_limit_bytes=12 * MIB),
        input_output_aliases={4: 0} if held else {},
    )(where, partial, arrived, other_weight, *held)


def partner(value, flip):
    count = lax.axis_size("seq")
    return lax.ppermute(value, "seq", [(i, i ^ flip) for i in range(count)])


def over_planes(value):
    groups = [[p * PLANE + r for p in range(PLANES)] for r in range(PLANE)]
    return lax.all_to_all(value, "seq", 0, 0, tiled=True, axis_index_groups=groups)


def shards(
    queries,
    key_rows,
    value_rows,
    token_rates,
    gate_fast,
    lift_fast,
    down_fast,
    memory_gain,
    out_weight,
):
    queries, key_rows, value_rows, token_rates, gate_fast, lift_fast, down_fast, out_weight = (
        pltpu.with_memory_space_constraint(x, pltpu.HBM)
        for x in (
            queries,
            key_rows,
            value_rows,
            token_rates,
            gate_fast,
            lift_fast,
            down_fast,
            out_weight,
        )
    )
    tokens_here = queries.shape[0]
    seq = lax.axis_index("seq")
    core = (seq % 2).astype(jnp.int32)
    head = lax.axis_index("head").astype(jnp.int32)
    where = jnp.stack([core, head])
    mirrored = jnp.stack([1 - core, head])
    has_edge = jnp.where(seq > 0, 1, 0).astype(jnp.int32).reshape(1)

    fast = (gate_fast, lift_fast, down_fast)
    tokens = (key_rows, value_rows, token_rates)
    grads_send = head_grads(mirrored, *tokens, *fast, BF)
    grads_got = partner(grads_send, 1)
    grads_mine = head_grads(where, *tokens, *fast, F32)

    count = lax.axis_size("seq")
    along = [(i, i + 1) for i in range(count - 1)]
    edge_keys = lax.ppermute(key_rows, "seq", along)
    other_columns, late, early = cut_blocks(where, out_weight, value_rows)
    edge_late = lax.ppermute(late, "seq", along)
    edge_early = lax.ppermute(early, "seq", along)
    pairs = [
        (group * count + i, (1 - group) * count + (i ^ 2)) for group in range(2) for i in range(count)
    ]
    other_first = lax.ppermute(other_columns, ("head", "seq"), pairs)
    other_last = partner(other_first, 1)

    chip_sum = add_blocks(grads_mine, grads_got)
    slices = over_planes(chip_sum.reshape(PLANES, -1, HEAD))
    part = sum_planes(slices)
    other = partner(part, 2)
    spread = add_and_repeat(part, other)
    grads = over_planes(spread).reshape(3 * HEAD, HEAD)

    weights_mine = renewed_weights(where, grads, *fast)
    weights_theirs = partner(weights_mine, 1)

    probability = pltpu.with_memory_space_constraint(
        probabilities(has_edge, queries, edge_keys, key_rows), pltpu.HBM
    )

    head_pair = [(0, 1), (1, 0)]
    half = tokens_here // 2
    plan = (
        (half, CHUNK, False),
        (half + CHUNK, CHUNK, False),
        (half, half, True),
        (0, half, False),
        (0, CHUNK, True),
        (CHUNK, CHUNK, True),
    )
    made, arrived, after = {}, {}, ()
    for start, rows, mirror in plan:
        piece = combined_piece(
            start,
            rows,
            mirror,
            where,
            queries,
            probability,
            weights_theirs if mirror else weights_mine,
            memory_gain,
            (edge_early, edge_late),
            value_rows,
            after,
        )
        after = (piece,)
        came = lax.ppermute(piece, "head", head_pair)
        for block in range(rows // CHUNK):
            made[mirror, start // CHUNK + block] = (piece, block)
            arrived[mirror, start // CHUNK + block] = (came, block)
    out, after = None, ()
    for pair in ((2, 3), (0, 1)):
        partials = {}
        for at in pair:
            operands = (made[False, at], made[True, at], arrived[False, at])
            partials[at] = project_chunk(where, operands, out_weight, other_first, after)
        for at in pair:
            out = finish_chunk(
                at, tokens_here, where, partials[at], *arrived[True, at], other_last, out
            )
        after = (out,)
    return out


def solution(mesh):
    return jax.shard_map(
        shards,
        mesh=mesh,
        in_specs=(
            P("seq", "head"),
            P("seq", "head"),
            P("seq", "head"),
            P("head", "seq"),
            P("head", None, None),
            P("head", None, None),
            P("head", None, None),
            P("head", None),
            P("head", None),
        ),
        out_specs=P("seq", "head"),
        check_vma=False,
    )
```
